32 devices in a mesh: groups: 2 (over x), blk: 8 (over z, y), split: 2 (over core).
Axes of the slice: x: 2, y: 2, z: 4, core: 2. Of those that a mesh axis runs over, the one named last changes fastest.
Arguments:
- embeddings: bfloat16 [32768, 768], P(('groups', 'blk', 'split')), parts along dimension 0, may hold values from -6 to 6
- cluster_of: int32 [32768], P(('groups', 'blk', 'split')), parts along dimension 0, may hold values from 0 to 15, as said below
- target_pos: int32 [32768], P(('groups', 'blk', 'split')), parts along dimension 0, may hold values from 0 to 16383, as said below
Outputs:
- best: float32 [32768], P(('groups', 'blk', 'split')), parts along dimension 0
The draws below stay inside these ranges and needn't reach their ends.
There are 2 independent parts, one for each index of `groups`. The reference program is written for one: setup_inputs(seed, part) draws one part's arguments, and reference() takes and returns one part's arrays. A program takes and returns all parts, laid end to end along the dimension named above; each array names one. Nothing has to cross between parts.
Inputs may be any that keep to these rules, and one draw needn't show every extreme that they name: `cluster_of`: ordering the members by target_pos lists cluster 0 first, then cluster 1 and so on, each cluster's members contiguous; every cluster has 2 to 4096 members and one has exactly 4096. `target_pos`: A permutation of the rows. For every aligned block of 1024 positions, each device's 1024 data-order rows hold exactly 64 of its positions.
All inputs are finite; a program needn't handle non-finite values.
Results may differ from the reference program's by a relative error of at most 0.0025.
Values may be sent and summed in bfloat16 or wider, within the bound.
A program may use at most 64 MiB of HBM per device.

```python
import jax
import jax.numpy as jnp
from jax import lax

D = 768
ROWS_DEV = 1024
DEVS_PART = 16
ROWS = 16384
CLUSTERS = 16
MOST = 4096


def layout_draw(key):
    key = jax.random.fold_in(key, 7)
    key_big, key_weights, key_blocks, key_shuffle = jax.random.split(key, 4)
    count = DEVS_PART
    rows = ROWS_DEV
    total = ROWS
    index = jnp.arange(CLUSTERS, dtype=jnp.int32)
    big = jax.random.randint(key_big, (), 0, CLUSTERS)
    weights = jax.random.randint(key_weights, (CLUSTERS,), 4, 8)
    others = index != big
    weights = jnp.where(others, weights, 0)
    spare = total - MOST - 2 * (CLUSTERS - 1)
    share = weights * spare // jnp.sum(weights)
    leftover = spare - jnp.sum(share)
    ranks = jnp.cumsum(others.astype(jnp.int32)) - 1
    extra = ((ranks < leftover) & others).astype(jnp.int32)
    sizes = jnp.where(others, 2 + share + extra, MOST).astype(jnp.int32)
    ends = jnp.cumsum(sizes)
    position = jnp.arange(total, dtype=jnp.int32)
    sorted_ids = jnp.sum((position[:, None] >= ends[None, :]).astype(jnp.int32), axis=1).astype(jnp.int32)
    perms = jax.vmap(lambda k: jax.random.permutation(k, rows))(jax.random.split(key_blocks, count))
    blocks = (jnp.arange(count, dtype=jnp.int32)[:, None] * rows + perms.astype(jnp.int32)).reshape(count, count, rows // count)
    by_source = jnp.transpose(blocks, (1, 0, 2)).reshape(count, rows)
    shuffle = jax.vmap(lambda k: jax.random.permutation(k, rows))(jax.random.split(key_shuffle, count))
    by_source = jnp.take_along_axis(by_source, shuffle.astype(jnp.int32), axis=1)
    target = by_source.reshape(total).astype(jnp.int32)
    return (sorted_ids[target], target)


def draw_cluster_of(key, part):
    return layout_draw(key)[0]


def draw_target_pos(key, part):
    return layout_draw(key)[1]


def block_scale(key, extent, shards, least, high):
    gain = 1.0
    for dim, parts in shards:
        steps = jax.random.uniform(jax.random.fold_in(jax.random.fold_in(key, 6), dim), (parts,), jnp.float32, least / len(shards), high / len(shards))
        gain = gain * jnp.repeat(jnp.exp(steps), extent[dim] // parts).reshape((-1,) + (1,) * (len(extent) - 1 - dim))
    return gain


def normal_values(key, dims, width, bound, cuts=(), held_as=jnp.bfloat16):
    loudness = block_scale(key, dims, cuts, -0.22, 0.18) if cuts else 1.0
    array = jax.random.normal(key, dims, jnp.float32) * width * loudness
    return jnp.minimum(jnp.maximum(array, -bound), bound).astype(held_as)


def setup_inputs(seed: int = 0, part: int = 0) -> dict:
    arg_keys = jax.random.split(jax.random.key(seed), 4)
    part_keys = jax.random.split(jax.random.fold_in(arg_keys[3], part), 4)
    embeddings = normal_values(part_keys[0], (ROWS, D), 1.0, 6.0, ((0, 16),))
    cluster_of = draw_cluster_of(jax.random.fold_in(jax.random.fold_in(arg_keys[3], part), 71), part)
    target_pos = draw_target_pos(jax.random.fold_in(jax.random.fold_in(arg_keys[3], part), 71), part)
    return {"embeddings": embeddings, "cluster_of": cluster_of, "target_pos": target_pos}


def reference(embeddings, cluster_of, target_pos):
    values = embeddings.astype(jnp.float32)
    unit = (values * lax.rsqrt(lax.optimization_barrier(jnp.sum(values * values, axis=1, keepdims=True)) + 1e-06)).astype(jnp.bfloat16)
    sorted_unit = jnp.zeros((ROWS, D), jnp.bfloat16).at[target_pos].set(unit)
    sorted_ids = jnp.zeros((ROWS,), jnp.int32).at[target_pos].set(cluster_of)
    margin = MOST
    span = ROWS_DEV + 2 * margin
    pad_unit = jnp.concatenate([jnp.zeros((margin, D), jnp.bfloat16), sorted_unit, jnp.zeros((margin, D), jnp.bfloat16)], axis=0)
    pad_ids = jnp.concatenate([jnp.full((margin,), -1, jnp.int32), sorted_ids, jnp.full((margin,), -1, jnp.int32)], axis=0)

    def one_block(block):
        start = (block * ROWS_DEV).astype(jnp.int32)
        rows = lax.dynamic_slice_in_dim(sorted_unit, start, ROWS_DEV, 0)
        row_ids = lax.dynamic_slice_in_dim(sorted_ids, start, ROWS_DEV, 0)
        window = lax.dynamic_slice_in_dim(pad_unit, start, span, 0)
        window_ids = lax.dynamic_slice_in_dim(pad_ids, start, span, 0)
        sims = jnp.dot(rows, window.T, preferred_element_type=jnp.float32)
        row_pos = start + jnp.arange(ROWS_DEV, dtype=jnp.int32)
        window_pos = start - margin + jnp.arange(span, dtype=jnp.int32)
        keep = (row_ids[:, None] == window_ids[None, :]) & (row_pos[:, None] != window_pos[None, :])
        return lax.optimization_barrier(jnp.max(jnp.where(keep, sims, -4.0), axis=1))
    best_sorted = lax.map(one_block, jnp.arange(ROWS // ROWS_DEV, dtype=jnp.int32)).reshape(ROWS)
    return best_sorted[target_pos]
```

```python
import functools

import jax
import jax.numpy as jnp
from jax import lax
from jax.experimental import pallas as pl
from jax.experimental.pallas import tpu as pltpu
from jax.sharding import PartitionSpec as P

MOST = 4096
FILL = -4.0
MESH = pl.DeviceIdType.MESH
F32 = jnp.float32
BF16 = jnp.bfloat16
I32 = jnp.int32


def nt(a, b):
    return lax.dot_general(a, b, (((1,), (1,)), ((), ())), preferred_element_type=F32)


def place(nq, at, s):
    if at > nq - 1 - at:
        at, s = nq - 1 - at, nq - 1 - s
    d = abs(s - at)
    if d > at:
        return at + d
    return 2 * d - 1 if s < at else 2 * d


def send_order(nq, q):
    up = list(range(2 * nq - 1, 2 * q + 1, -1))
    down = list(range(0, 2 * q))
    if len(up) > 4:
        up = up[:-3] + [2 * q + 3, 2 * q + 2, 2 * q + 4]
    if len(down) > 4:
        down = down[:-3] + [2 * q - 2, 2 * q - 1, 2 * q - 3]
    both = []
    for i in range(max(len(up), len(down))):
        both += up[i : i + 1] + down[i : i + 1]
    return both, [2 * q + 1, 2 * q]


def kernel(
    n, emb_in, cl_in, tp_in, out_ref,
    emb, cl, tp, packed, Q, E, idm, IDS, MSG, MSGR, best_m, best_e, racc, cacc, rid, qid,
    fetch_s, src_s, fx1_s, fx2_s, mr, er, y_s, y_r, c_s, c_r, d_s, d_r, ids_s, ids_r, msg_s, msg_r,
):
    nq = n // 4
    rows, width = emb.shape
    piece = rows // n
    cr = 2 * piece
    halves = 2 * nq
    wide = 4 * cr
    blk, split = lax.axis_index("blk"), lax.axis_index("split")
    me = blk * 2 + split
    q = blk // 2
    r = lax.rem(blk, 2) * 2 + split

    def dev(index):
        return {"blk": index // 2, "split": lax.rem(index, 2)}

    rc = lax.rem(blk, 2) * 2 + (1 - split)
    ry = lax.rem(r + 2, 4)
    rd = lax.rem(rc + 2, 4)
    core, across = 4 * q + rc, 4 * q + ry

    fetch = [
        pltpu.make_async_copy(src, dst, fetch_s.at[i])
        for i, (src, dst) in enumerate(((tp_in, tp), (cl_in, cl), (emb_in, emb)))
    ]
    for copy in fetch:
        copy.start()

    barrier = pltpu.get_barrier_semaphore()

    @pl.loop(1, n)
    def _(o):
        pl.semaphore_signal(
            barrier, inc=1, device_id=dev(lax.rem(me + o, n)), device_id_type=MESH
        )

    shift = rows.bit_length() - 1
    fetch[0].wait()
    dest = lax.shift_right_logical(tp[...], shift)
    hit = lax.broadcasted_iota(I32, (n, rows), 0) == dest
    hot = jnp.where(hit, 1.0, 0.0)
    lanes = 128
    before = jnp.where(
        lax.broadcasted_iota(I32, (lanes, lanes), 0) < lax.broadcasted_iota(I32, (lanes, lanes), 1), 1.0, 0.0
    ).astype(BF16)
    carry = jnp.zeros((n, 1), F32)
    ranks = []
    for b in range(rows // lanes):
        part = hot[:, b * lanes : (b + 1) * lanes]
        count = jnp.dot(part.astype(BF16), before, preferred_element_type=F32) + carry
        ranks.append(jnp.sum(part * count, axis=0, keepdims=True))
        carry = carry + jnp.sum(part, axis=1, keepdims=True)
    rank = jnp.concatenate(ranks, axis=1).astype(I32)
    key = dest * piece + rank
    fetch[1].wait()
    labels = jnp.broadcast_to(cl[...].astype(F32), (8, rows)).astype(BF16)
    fetch[2].wait()
    x = emb[...].astype(F32)
    unit = (x * lax.rsqrt(jnp.sum(x * x, axis=1, keepdims=True) + 1e-06)).astype(BF16)
    i0 = lax.broadcasted_iota(I32, (2 * cr, rows), 0)
    ids = []
    for w in range(nq):
        perm = jnp.where(i0 == key - 2 * cr * w, 1.0, 0.0).astype(BF16)
        packed[2 * w : 2 * w + 2] = (
            jnp.dot(perm, unit, preferred_element_type=F32).astype(BF16).reshape(2, cr, width)
        )
        ids.append(nt(labels, perm).astype(I32)[0:1])
    none = jnp.full((1, cr), -1, I32)
    padded = jnp.concatenate([none] + ids + [none], axis=1)
    for w in range(nq):
        idm[w] = padded[:, 2 * cr * w : 2 * cr * w + wide]

    pl.semaphore_wait(barrier, n - 1)

    def remote(src, dst, s_sem, r_sem, index):
        return pltpu.make_async_remote_copy(
            src_ref=src, dst_ref=dst, send_sem=s_sem, recv_sem=r_sem,
            device_id=dev(index), device_id_type=MESH,
        )

    def ids_copy(o):
        to = lax.rem(me + o, n)
        return remote(idm.at[to // 4], IDS.at[me], ids_s.at[o], ids_r.at[me], to)

    def ids_in(o):
        frm = lax.rem(me + o, n)
        return remote(idm.at[0], IDS.at[frm], ids_s.at[o], ids_r.at[frm], frm)

    @pl.loop(1, n)
    def _(o):
        ids_copy(o).start()

    flip = q > nq - 1 - q

    def source(j):
        m = jnp.minimum(q, nq - 1 - q)
        d = (j + 1) // 2
        near = jnp.where(lax.rem(j, 2) == 1, m - d, m + d)
        s = jnp.where(j <= 2 * m, near, j)
        return jnp.where(flip, nq - 1 - s, s)

    def early_slot(j):
        return 2 + (nq - 1 - j)

    def late_slot(at, s):
        turn = at > nq - 1 - at
        m = jnp.minimum(at, nq - 1 - at)
        sm = jnp.where(turn, nq - 1 - s, s)
        d = jnp.abs(sm - m)
        return nq + jnp.where(d <= m, jnp.where(sm < m, 2 * d - 1, 2 * d), m + d)

    def own_send(h, at):
        t, k = h // 2, h % 2
        e = t - 1 + 2 * k
        near = e if (at < t) == (e < t) else t
        if not 0 <= e < nq:
            near = t
        if at == t:
            near = e
        elif at == e:
            near = t
        if near == at or not 0 <= near < nq:
            return None
        if near == t:
            return remote(packed.at[h], Q.at[at, k, r], src_s.at[h], mr.at[k, at], 4 * t + r)
        j = place(nq, near, at)
        to = nq + j if at == t else early_slot(j)
        return remote(packed.at[h], E.at[to], src_s.at[h], er.at[to], 4 * near + r)

    def y_copy(k, s):
        return remote(Q.at[s, k, r], Q.at[s, k, r], y_s.at[k, s], y_r.at[k, s], across)

    def c_copy(k, s):
        return remote(Q.at[s, k, r], Q.at[s, k, r], c_s.at[k, s], c_r.at[k, s], core)

    def diag(k, s):
        there = Q.at[s, k, ry]
        return remote(there, there, d_s.at[k, s], d_r.at[k, s], core)

    def y_in(k, s):
        there = Q.at[s, k, ry]
        return remote(there, there, y_s.at[k, s], y_r.at[k, s], across)

    def c_in(k, s):
        there = Q.at[s, k, rc]
        return remote(there, there, c_s.at[k, s], c_r.at[k, s], core)

    def d_in(k, s):
        there = Q.at[s, k, rd]
        return remote(there, there, d_s.at[k, s], d_r.at[k, s], core)

    def mine_in(k, s):
        there = Q.at[s, k, r]
        return remote(there, there, y_s.at[k, s], mr.at[k, s], across)

    def ext_in(at):
        there = E.at[at]
        return remote(there, there, src_s.at[0], er.at[at], across)

    def below(s):
        return jnp.where(s < q, 1, 0)

    def inner(e):
        return jnp.where(e == 1, q < nq - 1, q > 0)

    def pass_mine(j):
        s = source(j)
        e = below(s)
        return remote(
            E.at[early_slot(j)], Q.at[s, 1 - e, r], fx1_s.at[s], mr.at[1 - e, s], me + 8 * e - 4
        )

    def pass_ext(j):
        s = source(j)
        e = below(s)
        to = late_slot(q + 2 * e - 1, s)
        return remote(Q.at[s, e, r], E.at[to], fx2_s.at[s], er.at[to], me + 8 * e - 4)

    def item(t):
        v = t - 3
        last = jnp.logical_or(t == 2, t == halves - 1)
        j = jnp.where(t < 2, 0, jnp.where(last, nq - 1, 1 + v // 2))
        second = jnp.where(t < 2, t, jnp.where(last, t != 2, lax.rem(v, 2)))
        s = source(j)
        e = below(s)
        return s, jnp.where(t < 2, t, jnp.where(second == 1, 1 - e, e))

    def place_of(t):
        return 0 if t < 2 else nq - 1 if t in (2, halves - 1) else 1 + (t - 3) // 2

    def start_sends(which):
        for at in range(nq):

            @pl.when(q == at)
            def _():
                for h in send_order(nq, at)[which]:
                    copy = own_send(h, at)
                    if copy is not None:
                        copy.start()

    for k in (0, 1):
        Q[q, k, r] = packed[2 * q + k]
        y_copy(k, q).start()
        c_copy(k, q).start()
    start_sends(0)
    E[0] = packed[jnp.maximum(2 * q - 1, 0)]
    E[1] = packed[jnp.minimum(2 * q + 2, halves - 1)]

    @pl.when(jnp.logical_or(q == 0, q == nq - 1))
    def _():
        for at in range(2, nq + 1):
            E[at] = jnp.zeros((cr, width), BF16)

    @pl.loop(1, n)
    def _(o):
        ids_in(o).wait_recv()

    IDS[me] = idm[q]

    for p in range(4):
        for s in range(nq):
            for k in (0, 1):
                qid[2 * s + k, 0:1, cr * p : cr * (p + 1)] = IDS[4 * s + p, :, cr * (k + 1) : cr * (k + 2)]

    def spread(row):
        return jnp.broadcast_to(row, (128, row.shape[1])).T

    for j in range(nq):
        rid[j] = spread(IDS[4 * source(j) + r, :, cr : 3 * cr])

    def ext_ids(s, upper):
        low, high = IDS[4 * s + r, :, 0:cr], IDS[4 * s + r, :, 3 * cr : 4 * cr]
        return jnp.where(upper == 1, high, low)

    ext_rows = [ext_ids(q, 0), ext_ids(q, 1)]
    for j in range(nq - 1, 0, -1):
        s = source(j)
        ext_rows.append(ext_ids(s, below(s)))
    for j in range(1, nq):
        s = source(j)
        ext_rows.append(ext_ids(s, 1 - below(s)))
    for g in range(nq):
        rid[nq + g] = spread(jnp.concatenate(ext_rows[2 * g : 2 * g + 2], axis=1))
    racc[...] = jnp.full(racc.shape, FILL, F32)
    cacc[...] = jnp.full(cacc.shape, FILL, F32)

    lane = lax.broadcasted_iota(I32, (2 * cr, 128), 1)
    sub = lax.broadcasted_iota(I32, (2 * cr, 128), 0)

    def scores_of(at, t):
        if at < nq:
            left = Q[source(at), :, r]
        else:
            left = E[2 * (at - nq) : 2 * (at - nq) + 2]
        s, k = item(t)
        return nt(left.reshape(2 * cr, width), Q[s, k].reshape(wide, width))

    def take(at, t, scores, same):
        s, k = item(t)
        at_b = 2 * s + k
        if same:
            own = jnp.logical_and(sub >= k * cr, sub < (k + 1) * cr)
            twin = jnp.where(own, sub + (r - k) * cr, -1) - lane
        ats = [slice(128 * w, 128 * (w + 1)) for w in range(wide // 128)]
        top = [cacc[at_b, :, at_w] for at_w in ats]
        step = min(64, 2 * cr)
        for x in range(0, 2 * cr, step):
            part = slice(x, x + step)
            col = rid[at, part]
            acc = racc[at, part]
            for w, at_w in enumerate(ats):
                keep = col == qid[at_b, 0:1, at_w]
                if same:
                    keep = jnp.logical_and(keep, twin[part] != 128 * w)
                block = jnp.where(keep, scores[part, at_w], FILL)
                acc = jnp.maximum(acc, block)
                top[w] = jnp.maximum(top[w], jnp.max(block.reshape(step // 8, 8, 128), axis=0))
            racc[at, part] = acc
        for w, at_w in enumerate(ats):
            cacc[at_b, :, at_w] = top[w]

    def tiles(work):
        work = [(at, t) for at, ts in work for t in ts]
        for x in range(0, len(work), 8):
            part = work[x : x + 8]
            scores = [scores_of(at, t) for at, t in part]
            for (at, t), one in zip(part, scores):
                take(at, t, one, at < nq and place_of(t) == at)

    half = nq // 2
    for i in range(halves + 2):
        if 2 <= i < halves:
            s, k = item(i)
            mine_in(k, s).wait_recv()
            y_copy(k, s).start()
            c_copy(k, s).start()
        if i == halves:
            ext_in(nq + 1).wait_recv()
            tiles([(nq - 1, range(halves - 2)), (nq + half, range(halves - 2))])
        if 1 <= i <= halves:
            s, k = item(i - 1)
            y_in(k, s).wait_recv()
            diag(k, s).start()
        if 2 <= i < halves:
            j = place_of(i)
            if i == 4 or (i != halves - 1 and j > 1 and (i == 2 or i % 2 == 1)):

                @pl.when(inner(below(source(j))))
                def _():
                    ext_in(early_slot(j)).wait_recv()
                    pass_mine(j).start()
                    if j > 1:
                        pass_ext(j).start()

            if i == 4:
                start_sends(1)

                @pl.when(inner(below(source(j))))
                def _():
                    pass_ext(j).start()

        if i >= 2:
            t = i - 2
            s, k = item(t)
            c_in(k, s).wait_recv()
            d_in(k, s).wait_recv()
            work = []
            if i == 3:
                work.append((0, (0, 1)))
            if i % 2 == 1:
                if 5 <= i < halves:
                    work.append(((i - 3) // 2, [u for u in range(t + 1) if u != 2]))
                work.append((nq, (t - 1, t)))
            elif 6 <= i:
                work.append(((i - 4) // 2, (t,)))
            if i >= halves - 2:
                first = i == halves - 2
                work += [(nq + g, range(t + 1) if first else (t,)) for g in range(1, half)]
            if i >= halves:
                work += [(nq - 1, (t,)), (nq + half, (t,))]
            tiles(work)
    for g in range(half + 1, nq):
        for one in (0, 1):
            ext_in(2 * g + one).wait_recv()
        tiles([(nq + g, range(halves))])

    best = jnp.max(racc[...].reshape(2 * nq * 2 * cr, 128).T, axis=0, keepdims=True)
    for at in range(halves):
        best_m[at] = best[:, at * cr : (at + 1) * cr]
        best_e[at] = best[:, (halves + at) * cr : (halves + at + 1) * cr]
    fill = jnp.full((1, cr), FILL, F32)
    for s in range(nq):
        e = below(s)
        own = q == s
        late = late_slot(q, s)
        early = early_slot(late - nq)
        low = best_e[jnp.where(own, 0, jnp.where(e == 1, late, early))]
        high = best_e[jnp.where(own, 1, jnp.where(e == 1, early, late))]
        for p in range(4):
            same = p == r
            found = [jnp.where(same, low, fill)]
            for k in (0, 1):
                column = jnp.max(cacc[2 * s + k, :, cr * p : cr * (p + 1)], axis=0, keepdims=True)
                mine = best_m[2 * jnp.where(own, 0, late - nq) + k]
                found.append(jnp.maximum(column, jnp.where(same, mine, fill)))
            found.append(jnp.where(same, high, fill))
            MSG[4 * s + p] = jnp.concatenate(found, axis=1)

    def msg_copy(o):
        to = lax.rem(me + o, n)
        return remote(MSG.at[to], MSGR.at[me], msg_s.at[o], msg_r.at[me], to)

    @pl.loop(1, n)
    def _(o):
        msg_copy(o).start()

    MSGR[me] = MSG[me]

    for at in range(nq):

        @pl.when(q == at)
        def _():
            for h in range(halves):
                copy = own_send(h, at)
                if copy is not None:
                    copy.wait_send()

    @pl.loop(1, n)
    def _(o):
        ids_copy(o).wait_send()

    @pl.loop(0, halves)
    def _(t):
        s, k = item(t)
        y_copy(k, s).wait_send()
        c_copy(k, s).wait_send()
        diag(k, s).wait_send()

    @pl.loop(1, nq)
    def _(j):
        @pl.when(inner(below(source(j))))
        def _():
            pass_mine(j).wait_send()
            pass_ext(j).wait_send()

    bits = cr.bit_length() - 1
    hot_l = jnp.where(
        lax.broadcasted_iota(I32, (cr, rows), 0) == (key & (cr - 1)), 1.0, 0.0
    ).astype(BF16)
    at_h = lax.broadcasted_iota(I32, (halves, rows), 0) == lax.shift_right_logical(key, bits)

    @pl.loop(1, n)
    def _(o):
        frm = lax.rem(me + o, n)
        remote(MSG.at[0], MSGR.at[frm], msg_s.at[o], msg_r.at[frm], frm).wait_recv()

    table = []
    for h in range(halves):
        t, k = h // 2, h % 2
        e = t - 1 + 2 * k
        found = MSGR[4 * t, :, (k + 1) * cr : (k + 2) * cr]
        for p in range(1, 4):
            found = jnp.maximum(found, MSGR[4 * t + p, :, (k + 1) * cr : (k + 2) * cr])
        if 0 <= e < nq:
            off = 3 * cr * (1 - k)
            found = jnp.maximum(found, MSGR[4 * e + r, :, off : off + cr])
        table.append(found)
    table = jnp.concatenate(table, axis=0)
    hi = table.astype(BF16)
    rest = table - hi.astype(F32)
    mid = rest.astype(BF16)
    low = (rest - mid.astype(F32)).astype(BF16)
    got = jnp.dot(hi, hot_l, preferred_element_type=F32)
    got += jnp.dot(mid, hot_l, preferred_element_type=F32)
    got += jnp.dot(low, hot_l, preferred_element_type=F32)
    out_ref[...] = jnp.max(jnp.where(at_h, got, FILL), axis=0, keepdims=True)

    @pl.loop(1, n)
    def _(o):
        msg_copy(o).wait_send()


def body(n, embeddings, cluster_of, target_pos):
    rows, width = embeddings.shape
    nq, cr = n // 4, 2 * rows // n
    assert MOST <= 4 * rows and n % 8 == 0
    dma = pltpu.SemaphoreType.DMA
    out = pl.pallas_call(
        functools.partial(kernel, n),
        out_shape=jax.ShapeDtypeStruct((1, rows), F32),
        in_specs=[pl.BlockSpec(memory_space=pl.ANY)] * 3,
        out_specs=pl.BlockSpec(memory_space=pltpu.VMEM),
        scratch_shapes=[
            pltpu.VMEM((rows, width), BF16),
            pltpu.VMEM((1, rows), I32),
            pltpu.VMEM((1, rows), I32),
            pltpu.VMEM((2 * nq, cr, width), BF16),
            pltpu.VMEM((nq, 2, 4, cr, width), BF16),
            pltpu.VMEM((2 * nq, cr, width), BF16),
            pltpu.VMEM((nq, 1, 4 * cr), I32),
            pltpu.VMEM((n, 1, 4 * cr), I32),
            pltpu.VMEM((n, 1, 4 * cr), F32),
            pltpu.VMEM((n, 1, 4 * cr), F32),
            pltpu.VMEM((2 * nq, 1, cr), F32),
            pltpu.VMEM((2 * nq, 1, cr), F32),
            pltpu.VMEM((2 * nq, 2 * cr, 128), F32),
            pltpu.VMEM((2 * nq, 8, 4 * cr), F32),
            pltpu.VMEM((2 * nq, 2 * cr, 128), I32),
            pltpu.VMEM((2 * nq, 8, 4 * cr), I32),
            dma((3,)), dma((2 * nq,)), dma((nq,)), dma((nq,)), dma((2, nq)), dma((2 * nq,)),
            dma((2, nq)), dma((2, nq)), dma((2, nq)), dma((2, nq)), dma((2, nq)), dma((2, nq)),
            dma((n,)), dma((n,)), dma((n,)), dma((n,)),
        ],
        compiler_params=pltpu.CompilerParams(
            collective_id=0, has_side_effects=True, vmem_limit_bytes=60 * 2**20
        ),
    )(embeddings, cluster_of.reshape(1, rows), target_pos.reshape(1, rows))
    return out.reshape(rows)


def solution(mesh):
    n = mesh.shape["blk"] * mesh.shape["split"]
    spec = P(("groups", "blk", "split"))
    return jax.shard_map(
        functools.partial(body, n),
        mesh=mesh,
        in_specs=(P(("groups", "blk", "split"), None), spec, spec),
        out_specs=spec,
        check_vma=False,
    )
```

```python
import functools

import jax
import jax.numpy as jnp
from jax import lax
from jax.experimental import pallas as pl
from jax.experimental.pallas import tpu as pltpu
from jax.sharding import PartitionSpec as P

MOST = 4096
FILL = -4.0
MESH = pl.DeviceIdType.MESH
F32 = jnp.float32
BF16 = jnp.bfloat16
I32 = jnp.int32


def nt(a, b):
    return lax.dot_general(a, b, (((1,), (1,)), ((), ())), preferred_element_type=F32)


def place(nq, at, s):
    if at > nq - 1 - at:
        at, s = nq - 1 - at, nq - 1 - s
    d = abs(s - at)
    if d > at:
        return at + d
    return 2 * d - 1 if s < at else 2 * d


def send_order(nq, q):
    up = list(range(2 * nq - 1, 2 * q + 1, -1))
    down = list(range(0, 2 * q))
    if len(up) > 4:
        up = up[:-3] + [2 * q + 3, 2 * q + 2, 2 * q + 4]
    if len(down) > 4:
        down = down[:-3] + [2 * q - 2, 2 * q - 1, 2 * q - 3]
    both = []
    for i in range(max(len(up), len(down))):
        both += up[i : i + 1] + down[i : i + 1]
    return both, [2 * q + 1, 2 * q]


def kernel(
    n, emb_in, cl_in, tp_in, out_ref,
    emb, cl, tp, packed, Q, E, idm, IDS, MSG, MSGR, best_m, best_e, racc, cacc, rid, qid,
    fetch_s, src_s, fx1_s, fx2_s, mr, er, y_s, y_r, c_s, c_r, d_s, d_r, ids_s, ids_r, msg_s, msg_r,
):
    nq = n // 4
    rows, width = emb.shape
    piece = rows // n
    cr = 2 * piece
    halves = 2 * nq
    wide = 4 * cr
    blk, split = lax.axis_index("blk"), lax.axis_index("split")
    me = blk * 2 + split
    q = blk // 2
    r = lax.rem(blk, 2) * 2 + split

    def dev(index):
        return {"blk": index // 2, "split": lax.rem(index, 2)}

    rc = lax.rem(blk, 2) * 2 + (1 - split)
    ry = lax.rem(r + 2, 4)
    rd = lax.rem(rc + 2, 4)
    core, across = 4 * q + rc, 4 * q + ry

    fetch = [
        pltpu.make_async_copy(src, dst, fetch_s.at[i])
        for i, (src, dst) in enumerate(((tp_in, tp), (cl_in, cl), (emb_in, emb)))
    ]
    for copy in fetch:
        copy.start()

    barrier = pltpu.get_barrier_semaphore()

    @pl.loop(1, n)
    def _(o):
        pl.semaphore_signal(
            barrier, inc=1, device_id=dev(lax.rem(me + o, n)), device_id_type=MESH
        )

    shift = rows.bit_length() - 1
    fetch[0].wait()
    dest = lax.shift_right_logical(tp[...], shift)
    hit = lax.broadcasted_iota(I32, (n, rows), 0) == dest
    hot = jnp.where(hit, 1.0, 0.0)
    lanes = 128
    before = jnp.where(
        lax.broadcasted_iota(I32, (lanes, lanes), 0) < lax.broadcasted_iota(I32, (lanes, lanes), 1), 1.0, 0.0
    ).astype(BF16)
    carry = jnp.zeros((n, 1), F32)
    ranks = []
    for b in range(rows // lanes):
        part = hot[:, b * lanes : (b + 1) * lanes]
        count = jnp.dot(part.astype(BF16), before, preferred_element_type=F32) + carry
        ranks.append(jnp.sum(part * count, axis=0, keepdims=True))
        carry = carry + jnp.sum(part, axis=1, keepdims=True)
    rank = jnp.concatenate(ranks, axis=1).astype(I32)
    key = dest * piece + rank
    fetch[1].wait()
    labels = jnp.broadcast_to(cl[...].astype(F32), (8, rows)).astype(BF16)
    fetch[2].wait()
    x = emb[...].astype(F32)
    unit = (x * lax.rsqrt(jnp.sum(x * x, axis=1, keepdims=True) + 1e-06)).astype(BF16)
    i0 = lax.broadcasted_iota(I32, (2 * cr, rows), 0)
    ids = []
    for w in range(nq):
        perm = jnp.where(i0 == key - 2 * cr * w, 1.0, 0.0).astype(BF16)
        packed[2 * w : 2 * w + 2] = (
            jnp.dot(perm, unit, preferred_element_type=F32).astype(BF16).reshape(2, cr, width)
        )
        ids.append(nt(labels, perm).astype(I32)[0:1])
    none = jnp.full((1, cr), -1, I32)
    padded = jnp.concatenate([none] + ids + [none], axis=1)
    for w in range(nq):
        idm[w] = padded[:, 2 * cr * w : 2 * cr * w + wide]

    pl.semaphore_wait(barrier, n - 1)

    def remote(src, dst, s_sem, r_sem, index):
        return pltpu.make_async_remote_copy(
            src_ref=src, dst_ref=dst, send_sem=s_sem, recv_sem=r_sem,
            device_id=dev(index), device_id_type=MESH,
        )

    def ids_copy(o):
        to = lax.rem(me + o, n)
        return remote(idm.at[to // 4], IDS.at[me], ids_s.at[o], ids_r.at[me], to)

    def ids_in(o):
        frm = lax.rem(me + o, n)
        return remote(idm.at[0], IDS.at[frm], ids_s.at[o], ids_r.at[frm], frm)

    @pl.loop(1, n)
    def _(o):
        ids_copy(o).start()

    flip = q > nq - 1 - q

    def source(j):
        m = jnp.minimum(q, nq - 1 - q)
        d = (j + 1) // 2
        near = jnp.where(lax.rem(j, 2) == 1, m - d, m + d)
        s = jnp.where(j <= 2 * m, near, j)
        return jnp.where(flip, nq - 1 - s, s)

    def early_slot(j):
        return 2 + (nq - 1 - j)

    def late_slot(at, s):
        turn = at > nq - 1 - at
        m = jnp.minimum(at, nq - 1 - at)
        sm = jnp.where(turn, nq - 1 - s, s)
        d = jnp.abs(sm - m)
        return nq + jnp.where(d <= m, jnp.where(sm < m, 2 * d - 1, 2 * d), m + d)

    def own_send(h, at):
        t, k = h // 2, h % 2
        e = t - 1 + 2 * k
        near = e if (at < t) == (e < t) else t
        if not 0 <= e < nq:
            near = t
        if at == t:
            near = e
        elif at == e:
            near = t
        if near == at or not 0 <= near < nq:
            return None
        if near == t:
            return remote(packed.at[h], Q.at[at, k, r], src_s.at[h], mr.at[k, at], 4 * t + r)
        j = place(nq, near, at)
        to = nq + j if at == t else early_slot(j)
        return remote(packed.at[h], E.at[to], src_s.at[h], er.at[to], 4 * near + r)

    def y_copy(k, s):
        return remote(Q.at[s, k, r], Q.at[s, k, r], y_s.at[k, s], y_r.at[k, s], across)

    def c_copy(k, s):
        return remote(Q.at[s, k, r], Q.at[s, k, r], c_s.at[k, s], c_r.at[k, s], core)

    def diag(k, s):
        there = Q.at[s, k, ry]
        return remote(there, there, d_s.at[k, s], d_r.at[k, s], core)

    def y_in(k, s):
        there = Q.at[s, k, ry]
        return remote(there, there, y_s.at[k, s], y_r.at[k, s], across)

    def c_in(k, s):
        there = Q.at[s, k, rc]
        return remote(there, there, c_s.at[k, s], c_r.at[k, s], core)

    def d_in(k, s):
        there = Q.at[s, k, rd]
        return remote(there, there, d_s.at[k, s], d_r.at[k, s], core)

    def mine_in(k, s):
        there = Q.at[s, k, r]
        return remote(there, there, y_s.at[k, s], mr.at[k, s], across)

    def ext_in(at):
        there = E.at[at]
        return remote(there, there, src_s.at[0], er.at[at], across)

    def below(s):
        return jnp.where(s < q, 1, 0)

    def inner(e):
        return jnp.where(e == 1, q < nq - 1, q > 0)

    def pass_mine(j):
        s = source(j)
        e = below(s)
        return remote(
            E.at[early_slot(j)], Q.at[s, 1 - e, r], fx1_s.at[s], mr.at[1 - e, s], me + 8 * e - 4
        )

    def pass_ext(j):
        s = source(j)
        e = below(s)
        to = late_slot(q + 2 * e - 1, s)
        return remote(Q.at[s, e, r], E.at[to], fx2_s.at[s], er.at[to], me + 8 * e - 4)

    def item(t):
        v = t - 3
        last = jnp.logical_or(t == 2, t == halves - 1)
        j = jnp.where(t < 2, 0, jnp.where(last, nq - 1, 1 + v // 2))
        second = jnp.where(t < 2, t, jnp.where(last, t != 2, lax.rem(v, 2)))
        s = source(j)
        e = below(s)
        return s, jnp.where(t < 2, t, jnp.where(second == 1, 1 - e, e))

    def place_of(t):
        return 0 if t < 2 else nq - 1 if t in (2, halves - 1) else 1 + (t - 3) // 2

    def start_sends(which):
        for at in range(nq):

            @pl.when(q == at)
            def _():
                for h in send_order(nq, at)[which]:
                    copy = own_send(h, at)
                    if copy is not None:
                        copy.start()

    for k in (0, 1):
        Q[q, k, r] = packed[2 * q + k]
        y_copy(k, q).start()
        c_copy(k, q).start()
    start_sends(0)
    E[0] = packed[jnp.maximum(2 * q - 1, 0)]
    E[1] = packed[jnp.minimum(2 * q + 2, halves - 1)]

    @pl.when(jnp.logical_or(q == 0, q == nq - 1))
    def _():
        for at in range(2, nq + 1):
            E[at] = jnp.zeros((cr, width), BF16)

    @pl.loop(1, n)
    def _(o):
        ids_in(o).wait_recv()

    IDS[me] = idm[q]

    for p in range(4):
        for s in range(nq):
            for k in (0, 1):
                qid[2 * s + k, 0:1, cr * p : cr * (p + 1)] = IDS[4 * s + p, :, cr * (k + 1) : cr * (k + 2)]

    def spread(row):
        return jnp.broadcast_to(row, (128, row.shape[1])).T

    for j in range(nq):
        rid[j] = spread(IDS[4 * source(j) + r, :, cr : 3 * cr])

    def ext_ids(s, upper):
        low, high = IDS[4 * s + r, :, 0:cr], IDS[4 * s + r, :, 3 * cr : 4 * cr]
        return jnp.where(upper == 1, high, low)

    ext_rows = [ext_ids(q, 0), ext_ids(q, 1)]
    for j in range(nq - 1, 0, -1):
        s = source(j)
        ext_rows.append(ext_ids(s, below(s)))
    for j in range(1, nq):
        s = source(j)
        ext_rows.append(ext_ids(s, 1 - below(s)))
    for g in range(nq):
        rid[nq + g] = spread(jnp.concatenate(ext_rows[2 * g : 2 * g + 2], axis=1))
    racc[...] = jnp.full(racc.shape, FILL, F32)
    cacc[...] = jnp.full(cacc.shape, FILL, F32)

    lane = lax.broadcasted_iota(I32, (2 * cr, 128), 1)
    sub = lax.broadcasted_iota(I32, (2 * cr, 128), 0)

    def scores_of(at, t):
        if at < nq:
            left = Q[source(at), :, r]
        else:
            left = E[2 * (at - nq) : 2 * (at - nq) + 2]
        s, k = item(t)
        return nt(left.reshape(2 * cr, width), Q[s, k].reshape(wide, width))

    def take(at, t, scores, same):
        s, k = item(t)
        at_b = 2 * s + k
        if same:
            own = jnp.logical_and(sub >= k * cr, sub < (k + 1) * cr)
            twin = jnp.where(own, sub + (r - k) * cr, -1) - lane
        ats = [slice(128 * w, 128 * (w + 1)) for w in range(wide // 128)]
        top = [cacc[at_b, :, at_w] for at_w in ats]
        step = min(64, 2 * cr)
        for x in range(0, 2 * cr, step):
            part = slice(x, x + step)
            col = rid[at, part]
            acc = racc[at, part]
            for w, at_w in enumerate(ats):
                keep = col == qid[at_b, 0:1, at_w]
                if same:
                    keep = jnp.logical_and(keep, twin[part] != 128 * w)
                block = jnp.where(keep, scores[part, at_w], FILL)
                acc = jnp.maximum(acc, block)
                top[w] = jnp.maximum(top[w], jnp.max(block.reshape(step // 8, 8, 128), axis=0))
            racc[at, part] = acc
        for w, at_w in enumerate(ats):
            cacc[at_b, :, at_w] = top[w]

    def tiles(work):
        work = [(at, t) for at, ts in work for t in ts]
        for x in range(0, len(work), 8):
            part = work[x : x + 8]
            scores = [scores_of(at, t) for at, t in part]
            for (at, t), one in zip(part, scores):
                take(at, t, one, at < nq and place_of(t) == at)

    def widen_next(copy, j):
        @pl.when(inner(below(source(j))))
        def _():
            if copy is pass_mine:
                ext_in(early_slot(j)).wait_recv()
            copy(j).start()

    half = nq // 2
    for i in range(halves + 2):
        if 2 <= i < halves:
            s, k = item(i)
            mine_in(k, s).wait_recv()
            y_copy(k, s).start()
            c_copy(k, s).start()
        if i == halves:
            tiles([(nq - 1, range(halves - 2))])
        if 1 <= i <= halves:
            s, k = item(i - 1)
            y_in(k, s).wait_recv()
            diag(k, s).start()
        if i == 2:
            widen_next(pass_mine, nq - 1)
        if i == 4:
            for j in range(nq - 2, 0, -1):
                widen_next(pass_mine, j)
            start_sends(1)
            widen_next(pass_ext, nq - 1)
            widen_next(pass_ext, 1)
        if 5 <= i < halves - 1 and i % 2 == 1:
            widen_next(pass_ext, i // 2)
        if i >= 2:
            t = i - 2
            s, k = item(t)
            c_in(k, s).wait_recv()
            d_in(k, s).wait_recv()
            work = []
            if i == 3:
                work.append((0, (0, 1)))
            if i % 2 == 1:
                if 5 <= i < halves:
                    work.append(((i - 3) // 2, [u for u in range(t + 1) if u != 2]))
                work.append((nq, (t - 1, t)))
            elif 6 <= i:
                work.append(((i - 4) // 2, (t,)))
            if i >= halves - 2:
                first = i == halves - 2
                work += [(nq + g, range(t + 1) if first else (t,)) for g in range(1, half)]
            if i >= halves:
                work.append((nq - 1, (t,)))
            if i > halves - 2:
                work.append((nq + half, (t,)))
            tiles(work)
            if i == halves - 2:
                ext_in(nq + 1).wait_recv()
                tiles([(nq + half, range(t + 1))])
    for g in range(half + 1, nq):
        for one in (0, 1):
            ext_in(2 * g + one).wait_recv()
        tiles([(nq + g, range(halves))])

    best = jnp.max(racc[...].reshape(2 * nq * 2 * cr, 128).T, axis=0, keepdims=True)
    for at in range(halves):
        best_m[at] = best[:, at * cr : (at + 1) * cr]
        best_e[at] = best[:, (halves + at) * cr : (halves + at + 1) * cr]
    fill = jnp.full((1, cr), FILL, F32)
    for s in range(nq):
        e = below(s)
        own = q == s
        late = late_slot(q, s)
        early = early_slot(late - nq)
        low = best_e[jnp.where(own, 0, jnp.where(e == 1, late, early))]
        high = best_e[jnp.where(own, 1, jnp.where(e == 1, early, late))]
        for p in range(4):
            same = p == r
            found = [jnp.where(same, low, fill)]
            for k in (0, 1):
                column = jnp.max(cacc[2 * s + k, :, cr * p : cr * (p + 1)], axis=0, keepdims=True)
                mine = best_m[2 * jnp.where(own, 0, late - nq) + k]
                found.append(jnp.maximum(column, jnp.where(same, mine, fill)))
            found.append(jnp.where(same, high, fill))
            MSG[4 * s + p] = jnp.concatenate(found, axis=1)

    def msg_copy(o):
        to = lax.rem(me + o, n)
        return remote(MSG.at[to], MSGR.at[me], msg_s.at[o], msg_r.at[me], to)

    @pl.loop(1, n)
    def _(o):
        msg_copy(o).start()

    MSGR[me] = MSG[me]

    for at in range(nq):

        @pl.when(q == at)
        def _():
            for h in range(halves):
                copy = own_send(h, at)
                if copy is not None:
                    copy.wait_send()

    @pl.loop(1, n)
    def _(o):
        ids_copy(o).wait_send()

    @pl.loop(0, halves)
    def _(t):
        s, k = item(t)
        y_copy(k, s).wait_send()
        c_copy(k, s).wait_send()
        diag(k, s).wait_send()

    @pl.loop(1, nq)
    def _(j):
        @pl.when(inner(below(source(j))))
        def _():
            pass_mine(j).wait_send()
            pass_ext(j).wait_send()

    bits = cr.bit_length() - 1
    hot_l = jnp.where(
        lax.broadcasted_iota(I32, (cr, rows), 0) == (key & (cr - 1)), 1.0, 0.0
    ).astype(BF16)
    at_h = lax.broadcasted_iota(I32, (halves, rows), 0) == lax.shift_right_logical(key, bits)

    @pl.loop(1, n)
    def _(o):
        frm = lax.rem(me + o, n)
        remote(MSG.at[0], MSGR.at[frm], msg_s.at[o], msg_r.at[frm], frm).wait_recv()

    table = []
    for h in range(halves):
        t, k = h // 2, h % 2
        e = t - 1 + 2 * k
        found = MSGR[4 * t, :, (k + 1) * cr : (k + 2) * cr]
        for p in range(1, 4):
            found = jnp.maximum(found, MSGR[4 * t + p, :, (k + 1) * cr : (k + 2) * cr])
        if 0 <= e < nq:
            off = 3 * cr * (1 - k)
            found = jnp.maximum(found, MSGR[4 * e + r, :, off : off + cr])
        table.append(found)
    table = jnp.concatenate(table, axis=0)
    hi = table.astype(BF16)
    rest = table - hi.astype(F32)
    mid = rest.astype(BF16)
    low = (rest - mid.astype(F32)).astype(BF16)
    got = jnp.dot(hi, hot_l, preferred_element_type=F32)
    got += jnp.dot(mid, hot_l, preferred_element_type=F32)
    got += jnp.dot(low, hot_l, preferred_element_type=F32)
    out_ref[...] = jnp.max(jnp.where(at_h, got, FILL), axis=0, keepdims=True)

    @pl.loop(1, n)
    def _(o):
        msg_copy(o).wait_send()


def body(n, embeddings, cluster_of, target_pos):
    rows, width = embeddings.shape
    nq, cr = n // 4, 2 * rows // n
    assert MOST <= 4 * rows and n % 8 == 0
    dma = pltpu.SemaphoreType.DMA
    out = pl.pallas_call(
        functools.partial(kernel, n),
        out_shape=jax.ShapeDtypeStruct((1, rows), F32),
        in_specs=[pl.BlockSpec(memory_space=pl.ANY)] * 3,
        out_specs=pl.BlockSpec(memory_space=pltpu.VMEM),
        scratch_shapes=[
            pltpu.VMEM((rows, width), BF16),
            pltpu.VMEM((1, rows), I32),
            pltpu.VMEM((1, rows), I32),
            pltpu.VMEM((2 * nq, cr, width), BF16),
            pltpu.VMEM((nq, 2, 4, cr, width), BF16),
            pltpu.VMEM((2 * nq, cr, width), BF16),
            pltpu.VMEM((nq, 1, 4 * cr), I32),
            pltpu.VMEM((n, 1, 4 * cr), I32),
            pltpu.VMEM((n, 1, 4 * cr), F32),
            pltpu.VMEM((n, 1, 4 * cr), F32),
            pltpu.VMEM((2 * nq, 1, cr), F32),
            pltpu.VMEM((2 * nq, 1, cr), F32),
            pltpu.VMEM((2 * nq, 2 * cr, 128), F32),
            pltpu.VMEM((2 * nq, 8, 4 * cr), F32),
            pltpu.VMEM((2 * nq, 2 * cr, 128), I32),
            pltpu.VMEM((2 * nq, 8, 4 * cr), I32),
            dma((3,)), dma((2 * nq,)), dma((nq,)), dma((nq,)), dma((2, nq)), dma((2 * nq,)),
            dma((2, nq)), dma((2, nq)), dma((2, nq)), dma((2, nq)), dma((2, nq)), dma((2, nq)),
            dma((n,)), dma((n,)), dma((n,)), dma((n,)),
        ],
        compiler_params=pltpu.CompilerParams(
            collective_id=0, has_side_effects=True, vmem_limit_bytes=60 * 2**20
        ),
    )(embeddings, cluster_of.reshape(1, rows), target_pos.reshape(1, rows))
    return out.reshape(rows)


def solution(mesh):
    n = mesh.shape["blk"] * mesh.shape["split"]
    spec = P(("groups", "blk", "split"))
    return jax.shard_map(
        functools.partial(body, n),
        mesh=mesh,
        in_specs=(P(("groups", "blk", "split"), None), spec, spec),
        out_specs=spec,
        check_vma=False,
    )
```

```python
import functools

import jax
import jax.numpy as jnp
from jax import lax
from jax.experimental import pallas as pl
from jax.experimental.pallas import tpu as pltpu
from jax.sharding import PartitionSpec as P

MOST = 4096
FILL = -4.0
MESH = pl.DeviceIdType.MESH
F32 = jnp.float32
BF16 = jnp.bfloat16
I32 = jnp.int32


def nt(a, b):
    return lax.dot_general(a, b, (((1,), (1,)), ((), ())), preferred_element_type=F32)


def place(nq, at, s):
    if at > nq - 1 - at:
        at, s = nq - 1 - at, nq - 1 - s
    d = abs(s - at)
    if d > at:
        return at + d
    return 2 * d - 1 if s < at else 2 * d


def send_order(nq, q):
    up = list(range(2 * nq - 1, 2 * q + 1, -1))
    down = list(range(0, 2 * q))
    if len(up) > 4:
        up = up[:-3] + [2 * q + 3, 2 * q + 2, 2 * q + 4]
    if len(down) > 4:
        down = down[:-3] + [2 * q - 2, 2 * q - 1, 2 * q - 3]
    return up, down


def windows(nq, q):
    return list(range(nq)) if q >= nq // 2 else list(range(nq - 1, -1, -1))


def sends_after(nq, q, step):
    def ready(step):
        packed = windows(nq, q)[: step + 1]
        out = []
        for way in send_order(nq, q):
            for h in way:
                if h // 2 not in packed:
                    break
                out.append(h)
        return out

    before = ready(step - 1) if step else []
    return [h for h in ready(step) if h not in before]


def kernel(
    n, emb_in, cl_in, tp_in, out_ref,
    emb, cl, tp, packed, Q, E, idm, IDS, MSG, MSGR, top, racc, cacc, rid, qid,
    fetch_s, src_s, fx1_s, fx2_s, mr, er, y_s, y_r, c_s, c_r, d_s, d_r, ids_s, ids_r, msg_s, msg_r,
):
    nq = n // 4
    rows, width = emb.shape
    piece = rows // n
    cr = 2 * piece
    halves = 2 * nq
    wide = 4 * cr
    blk, split = lax.axis_index("blk"), lax.axis_index("split")
    me = blk * 2 + split
    q = blk // 2
    r = lax.rem(blk, 2) * 2 + split

    def dev(index):
        return {"blk": index // 2, "split": lax.rem(index, 2)}

    rc = lax.rem(blk, 2) * 2 + (1 - split)
    ry = lax.rem(r + 2, 4)
    rd = lax.rem(rc + 2, 4)
    core, across = 4 * q + rc, 4 * q + ry

    fetch = [
        pltpu.make_async_copy(src, dst, fetch_s.at[i])
        for i, (src, dst) in enumerate(((tp_in, tp), (cl_in, cl), (emb_in, emb)))
    ]
    for copy in fetch:
        copy.start()

    barrier = pltpu.get_barrier_semaphore()

    @pl.loop(1, n)
    def _(o):
        pl.semaphore_signal(
            barrier, inc=1, device_id=dev(lax.rem(me + o, n)), device_id_type=MESH
        )

    shift = rows.bit_length() - 1
    fetch[0].wait()
    dest = lax.shift_right_logical(tp[...], shift)
    hit = lax.broadcasted_iota(I32, (n, rows), 0) == dest
    hot = jnp.where(hit, 1.0, 0.0)
    lanes = 128
    before = jnp.where(
        lax.broadcasted_iota(I32, (lanes, lanes), 0) < lax.broadcasted_iota(I32, (lanes, lanes), 1), 1.0, 0.0
    ).astype(BF16)
    carry = jnp.zeros((n, 1), F32)
    ranks = []
    for b in range(rows // lanes):
        some = hot[:, b * lanes : (b + 1) * lanes]
        count = jnp.dot(some.astype(BF16), before, preferred_element_type=F32) + carry
        ranks.append(jnp.sum(some * count, axis=0, keepdims=True))
        carry = carry + jnp.sum(some, axis=1, keepdims=True)
    rank = jnp.concatenate(ranks, axis=1).astype(I32)
    key = dest * piece + rank
    i0 = lax.broadcasted_iota(I32, (2 * cr, rows), 0)

    def permutation(w):
        return jnp.where(i0 == key - 2 * cr * w, 1.0, 0.0).astype(BF16)

    fetch[1].wait()
    labels = jnp.broadcast_to(cl[...].astype(F32), (8, rows)).astype(BF16)
    none = jnp.full((1, cr), -1, I32)
    padded = jnp.concatenate(
        [none] + [nt(labels, permutation(w)).astype(I32)[0:1] for w in range(nq)] + [none], axis=1
    )
    for w in range(nq):
        idm[w] = padded[:, 2 * cr * w : 2 * cr * w + wide]

    def remote(src, dst, s_sem, r_sem, index):
        return pltpu.make_async_remote_copy(
            src_ref=src, dst_ref=dst, send_sem=s_sem, recv_sem=r_sem,
            device_id=dev(index), device_id_type=MESH,
        )

    def ids_copy(o):
        to = lax.rem(me + o, n)
        return remote(idm.at[to // 4], IDS.at[me], ids_s.at[o], ids_r.at[me], to)

    def ids_in(o):
        frm = lax.rem(me + o, n)
        return remote(idm.at[0], IDS.at[frm], ids_s.at[o], ids_r.at[frm], frm)

    flip = q > nq - 1 - q

    def source(j):
        m = jnp.minimum(q, nq - 1 - q)
        d = (j + 1) // 2
        near = jnp.where(lax.rem(j, 2) == 1, m - d, m + d)
        s = jnp.where(j <= 2 * m, near, j)
        return jnp.where(flip, nq - 1 - s, s)

    def early_slot(j):
        return 2 + (nq - 1 - j)

    def late_slot(at, s):
        turn = at > nq - 1 - at
        m = jnp.minimum(at, nq - 1 - at)
        sm = jnp.where(turn, nq - 1 - s, s)
        d = jnp.abs(sm - m)
        return nq + jnp.where(d <= m, jnp.where(sm < m, 2 * d - 1, 2 * d), m + d)

    def own_send(h, at):
        t, k = h // 2, h % 2
        e = t - 1 + 2 * k
        near = e if (at < t) == (e < t) else t
        if not 0 <= e < nq:
            near = t
        if at == t:
            near = e
        elif at == e:
            near = t
        if near == at or not 0 <= near < nq:
            return None
        if near == t:
            return remote(packed.at[h], Q.at[at, k, r], src_s.at[h], mr.at[k, at], 4 * t + r)
        j = place(nq, near, at)
        to = nq + j if at == t else early_slot(j)
        return remote(packed.at[h], E.at[to], src_s.at[h], er.at[to], 4 * near + r)

    def y_copy(k, s):
        return remote(Q.at[s, k, r], Q.at[s, k, r], y_s.at[k, s], y_r.at[k, s], across)

    def c_copy(k, s):
        return remote(Q.at[s, k, r], Q.at[s, k, r], c_s.at[k, s], c_r.at[k, s], core)

    def diag(k, s):
        there = Q.at[s, k, ry]
        return remote(there, there, d_s.at[k, s], d_r.at[k, s], core)

    def y_in(k, s):
        there = Q.at[s, k, ry]
        return remote(there, there, y_s.at[k, s], y_r.at[k, s], across)

    def c_in(k, s):
        there = Q.at[s, k, rc]
        return remote(there, there, c_s.at[k, s], c_r.at[k, s], core)

    def d_in(k, s):
        there = Q.at[s, k, rd]
        return remote(there, there, d_s.at[k, s], d_r.at[k, s], core)

    def mine_in(k, s):
        there = Q.at[s, k, r]
        return remote(there, there, y_s.at[k, s], mr.at[k, s], across)

    def ext_in(at):
        there = E.at[at]
        return remote(there, there, src_s.at[0], er.at[at], across)

    def below(s):
        return jnp.where(s < q, 1, 0)

    def inner(e):
        return jnp.where(e == 1, q < nq - 1, q > 0)

    def pass_mine(j):
        s = source(j)
        e = below(s)
        return remote(
            E.at[early_slot(j)], Q.at[s, 1 - e, r], fx1_s.at[s], mr.at[1 - e, s], me + 8 * e - 4
        )

    def pass_ext(j):
        s = source(j)
        e = below(s)
        to = late_slot(q + 2 * e - 1, s)
        return remote(Q.at[s, e, r], E.at[to], fx2_s.at[s], er.at[to], me + 8 * e - 4)

    def item(t):
        v = t - 3
        last = jnp.logical_or(t == 2, t == halves - 1)
        j = jnp.where(t < 2, 0, jnp.where(last, nq - 1, 1 + v // 2))
        second = jnp.where(t < 2, t, jnp.where(last, t != 2, lax.rem(v, 2)))
        s = source(j)
        e = below(s)
        return s, jnp.where(t < 2, t, jnp.where(second == 1, 1 - e, e))

    def place_of(t):
        return 0 if t < 2 else nq - 1 if t in (2, halves - 1) else 1 + (t - 3) // 2

    def start_all(at, halves_out):
        for h in halves_out:
            copy = own_send(h, at)
            if copy is not None:
                copy.start()

    for step in range(nq):
        w = jnp.where(q >= nq // 2, step, nq - 1 - step)
        if step == 0:
            fetch[2].wait()
            pl.semaphore_wait(barrier, n - 1)
            for o in range(1, n):
                ids_copy(o).start()
        x = jnp.dot(permutation(w), emb[...], preferred_element_type=F32)
        x = x * lax.rsqrt(jnp.sum(x * x, axis=1, keepdims=True) + 1e-06)
        packed[pl.ds(2 * w, 2)] = x.astype(BF16).reshape(2, cr, width)
        for at in range(nq):

            @pl.when(q == at)
            def _():
                start_all(at, sends_after(nq, at, step))
                if windows(nq, at)[step] == at:
                    for k in (0, 1):
                        Q[at, k, r] = packed[2 * at + k]
                        y_copy(k, at).start()
                        c_copy(k, at).start()

    E[0] = packed[jnp.maximum(2 * q - 1, 0)]
    E[1] = packed[jnp.minimum(2 * q + 2, halves - 1)]

    @pl.when(jnp.logical_or(q == 0, q == nq - 1))
    def _():
        for at in range(2, nq + 1):
            E[at] = jnp.zeros((cr, width), BF16)

    @pl.loop(1, n)
    def _(o):
        ids_in(o).wait_recv()

    IDS[me] = idm[q]

    for p in range(4):
        for s in range(nq):
            for k in (0, 1):
                qid[2 * s + k, 0:1, cr * p : cr * (p + 1)] = IDS[4 * s + p, :, cr * (k + 1) : cr * (k + 2)]

    def spread(row):
        return jnp.broadcast_to(row, (128, row.shape[1])).T

    for j in range(nq):
        rid[j] = spread(IDS[4 * source(j) + r, :, cr : 3 * cr])

    def ext_ids(s, upper):
        low, high = IDS[4 * s + r, :, 0:cr], IDS[4 * s + r, :, 3 * cr : 4 * cr]
        return jnp.where(upper == 1, high, low)

    ext_rows = [ext_ids(q, 0), ext_ids(q, 1)]
    for j in range(nq - 1, 0, -1):
        s = source(j)
        ext_rows.append(ext_ids(s, below(s)))
    for j in range(1, nq):
        s = source(j)
        ext_rows.append(ext_ids(s, 1 - below(s)))
    for g in range(nq):
        rid[nq + g] = spread(jnp.concatenate(ext_rows[2 * g : 2 * g + 2], axis=1))
    racc[...] = jnp.full(racc.shape, FILL, F32)
    cacc[...] = jnp.full(cacc.shape, FILL, F32)

    lane = lax.broadcasted_iota(I32, (2 * cr, 128), 1)
    sub = lax.broadcasted_iota(I32, (2 * cr, 128), 0)

    def scores_of(at, t, side):
        if at < nq:
            left = Q[source(at), :, r].reshape(2 * cr, width)
        elif side is None:
            left = E[2 * (at - nq) : 2 * (at - nq) + 2].reshape(2 * cr, width)
        else:
            left = E[2 * (at - nq) + side]
        s, k = item(t)
        return nt(left, Q[s, k].reshape(wide, width))

    def take(at, t, scores, same, side):
        s, k = item(t)
        at_b = 2 * s + k
        if same:
            own = jnp.logical_and(sub >= k * cr, sub < (k + 1) * cr)
            twin = jnp.where(own, sub + (r - k) * cr, -1) - lane
        ats = [slice(128 * w, 128 * (w + 1)) for w in range(wide // 128)]
        high = [cacc[at_b, :, at_w] for at_w in ats]
        step = min(64, cr)
        for x in range(0, scores.shape[0], step):
            base = x if side is None else side * cr + x
            part, there = slice(base, base + step), slice(x, x + step)
            col = rid[at, part]
            acc = racc[at, part]
            for w, at_w in enumerate(ats):
                keep = col == qid[at_b, 0:1, at_w]
                if same:
                    keep = jnp.logical_and(keep, twin[part] != 128 * w)
                block = jnp.where(keep, scores[there, at_w], FILL)
                acc = jnp.maximum(acc, block)
                high[w] = jnp.maximum(high[w], jnp.max(block.reshape(step // 8, 8, 128), axis=0))
            racc[at, part] = acc
        for w, at_w in enumerate(ats):
            cacc[at_b, :, at_w] = high[w]

    def tiles(work, side=None):
        work = [(at, t) for at, ts in work for t in ts]
        for x in range(0, len(work), 8):
            part = work[x : x + 8]
            scores = [scores_of(at, t, side) for at, t in part]
            for (at, t), one in zip(part, scores):
                take(at, t, one, at < nq and place_of(t) == at, side)

    def widen_next(copy, j):
        @pl.when(inner(below(source(j))))
        def _():
            if copy is pass_mine:
                ext_in(early_slot(j)).wait_recv()
            copy(j).start()

    half = nq // 2
    for i in range(halves + 2):
        if 2 <= i < halves:
            s, k = item(i)
            mine_in(k, s).wait_recv()
            y_copy(k, s).start()
            c_copy(k, s).start()
        if i == halves:
            tiles([(nq - 1, range(halves - 2))])
        if 1 <= i <= halves:
            s, k = item(i - 1)
            y_in(k, s).wait_recv()
            diag(k, s).start()
        if i == 2:
            widen_next(pass_mine, nq - 1)
        if i == 4:
            for j in range(nq - 2, 0, -1):
                widen_next(pass_mine, j)
            for at in range(nq):

                @pl.when(q == at)
                def _():
                    start_all(at, (2 * at + 1, 2 * at))

            widen_next(pass_ext, nq - 1)
            widen_next(pass_ext, 1)
        if 5 <= i < halves - 1 and i % 2 == 1:
            widen_next(pass_ext, i // 2)
        if i >= 2:
            t = i - 2
            s, k = item(t)
            c_in(k, s).wait_recv()
            d_in(k, s).wait_recv()
            work = []
            if i == 3:
                work.append((0, (0, 1)))
            if i % 2 == 1:
                if 5 <= i < halves:
                    work.append(((i - 3) // 2, [u for u in range(t + 1) if u != 2]))
                work.append((nq, (t - 1, t)))
            elif 6 <= i:
                work.append(((i - 4) // 2, (t,)))
            if i >= halves - 2:
                first = i == halves - 2
                work += [(nq + g, range(t + 1) if first else (t,)) for g in range(1, half)]
            if i >= halves:
                work.append((nq - 1, (t,)))
            if i > halves - 2:
                work.append((nq + half, (t,)))
            tiles(work)
            if i == halves - 2:
                ext_in(nq + 1).wait_recv()
                tiles([(nq + half, range(t + 1))])
    def settle(first, last):
        best = jnp.max(racc[first:last].reshape(2 * (last - first) * cr, 128).T, axis=0, keepdims=True)
        for at in range(2 * (last - first)):
            top[2 * first + at] = best[:, at * cr : (at + 1) * cr]

    settle(0, nq + half + 1)
    for g in range(half + 1, nq):
        for side in (0, 1):
            ext_in(2 * g + side).wait_recv()
        tiles([(nq + g, range(halves))])

    settle(nq + half + 1, 2 * nq)
    fill = jnp.full((1, cr), FILL, F32)
    for s in range(nq):
        e = below(s)
        own = q == s
        late = late_slot(q, s)
        early = early_slot(late - nq)
        low = top[halves + jnp.where(own, 0, jnp.where(e == 1, late, early))]
        high = top[halves + jnp.where(own, 1, jnp.where(e == 1, early, late))]
        for p in range(4):
            same = p == r
            found = [jnp.where(same, low, fill)]
            for k in (0, 1):
                column = jnp.max(cacc[2 * s + k, :, cr * p : cr * (p + 1)], axis=0, keepdims=True)
                mine = top[2 * jnp.where(own, 0, late - nq) + k]
                found.append(jnp.maximum(column, jnp.where(same, mine, fill)))
            found.append(jnp.where(same, high, fill))
            MSG[4 * s + p] = jnp.concatenate(found, axis=1)

    def msg_copy(o):
        to = lax.rem(me + o, n)
        return remote(MSG.at[to], MSGR.at[me], msg_s.at[o], msg_r.at[me], to)

    @pl.loop(1, n)
    def _(o):
        msg_copy(o).start()

    MSGR[me] = MSG[me]

    for at in range(nq):

        @pl.when(q == at)
        def _():
            for h in range(halves):
                copy = own_send(h, at)
                if copy is not None:
                    copy.wait_send()

    @pl.loop(1, n)
    def _(o):
        ids_copy(o).wait_send()

    @pl.loop(0, halves)
    def _(t):
        s, k = item(t)
        y_copy(k, s).wait_send()
        c_copy(k, s).wait_send()
        diag(k, s).wait_send()

    @pl.loop(1, nq)
    def _(j):
        @pl.when(inner(below(source(j))))
        def _():
            pass_mine(j).wait_send()
            pass_ext(j).wait_send()

    bits = cr.bit_length() - 1
    hot_l = jnp.where(
        lax.broadcasted_iota(I32, (cr, rows), 0) == (key & (cr - 1)), 1.0, 0.0
    ).astype(BF16)
    at_h = lax.broadcasted_iota(I32, (halves, rows), 0) == lax.shift_right_logical(key, bits)

    @pl.loop(1, n)
    def _(o):
        frm = lax.rem(me + o, n)
        remote(MSG.at[0], MSGR.at[frm], msg_s.at[o], msg_r.at[frm], frm).wait_recv()

    table = []
    for h in range(halves):
        t, k = h // 2, h % 2
        e = t - 1 + 2 * k
        found = MSGR[4 * t, :, (k + 1) * cr : (k + 2) * cr]
        for p in range(1, 4):
            found = jnp.maximum(found, MSGR[4 * t + p, :, (k + 1) * cr : (k + 2) * cr])
        if 0 <= e < nq:
            off = 3 * cr * (1 - k)
            found = jnp.maximum(found, MSGR[4 * e + r, :, off : off + cr])
        table.append(found)
    table = jnp.concatenate(table, axis=0)
    hi = table.astype(BF16)
    rest = table - hi.astype(F32)
    mid = rest.astype(BF16)
    low = (rest - mid.astype(F32)).astype(BF16)
    got = jnp.dot(hi, hot_l, preferred_element_type=F32)
    got += jnp.dot(mid, hot_l, preferred_element_type=F32)
    got += jnp.dot(low, hot_l, preferred_element_type=F32)
    out_ref[...] = jnp.max(jnp.where(at_h, got, FILL), axis=0, keepdims=True)

    @pl.loop(1, n)
    def _(o):
        msg_copy(o).wait_send()


def body(n, embeddings, cluster_of, target_pos):
    rows, width = embeddings.shape
    nq, cr = n // 4, 2 * rows // n
    assert MOST <= 4 * rows and n % 8 == 0
    dma = pltpu.SemaphoreType.DMA
    out = pl.pallas_call(
        functools.partial(kernel, n),
        out_shape=jax.ShapeDtypeStruct((1, rows), F32),
        in_specs=[pl.BlockSpec(memory_space=pl.ANY)] * 3,
        out_specs=pl.BlockSpec(memory_space=pltpu.VMEM),
        scratch_shapes=[
            pltpu.VMEM((rows, width), BF16),
            pltpu.VMEM((1, rows), I32),
            pltpu.VMEM((1, rows), I32),
            pltpu.VMEM((2 * nq, cr, width), BF16),
            pltpu.VMEM((nq, 2, 4, cr, width), BF16),
            pltpu.VMEM((2 * nq, cr, width), BF16),
            pltpu.VMEM((nq, 1, 4 * cr), I32),
            pltpu.VMEM((n, 1, 4 * cr), I32),
            pltpu.VMEM((n, 1, 4 * cr), F32),
            pltpu.VMEM((n, 1, 4 * cr), F32),
            pltpu.VMEM((4 * nq, 1, cr), F32),
            pltpu.VMEM((2 * nq, 2 * cr, 128), F32),
            pltpu.VMEM((2 * nq, 8, 4 * cr), F32),
            pltpu.VMEM((2 * nq, 2 * cr, 128), I32),
            pltpu.VMEM((2 * nq, 8, 4 * cr), I32),
            dma((3,)), dma((2 * nq,)), dma((nq,)), dma((nq,)), dma((2, nq)), dma((2 * nq,)),
            dma((2, nq)), dma((2, nq)), dma((2, nq)), dma((2, nq)), dma((2, nq)), dma((2, nq)),
            dma((n,)), dma((n,)), dma((n,)), dma((n,)),
        ],
        compiler_params=pltpu.CompilerParams(
            collective_id=0, has_side_effects=True, vmem_limit_bytes=60 * 2**20
        ),
    )(embeddings, cluster_of.reshape(1, rows), target_pos.reshape(1, rows))
    return out.reshape(rows)


def solution(mesh):
    n = mesh.shape["blk"] * mesh.shape["split"]
    spec = P(("groups", "blk", "split"))
    return jax.shard_map(
        functools.partial(body, n),
        mesh=mesh,
        in_specs=(P(("groups", "blk", "split"), None), spec, spec),
        out_specs=spec,
        check_vma=False,
    )
```

```python
import functools

import jax
import jax.numpy as jnp
from jax import lax
from jax.experimental import pallas as pl
from jax.experimental.pallas import tpu as pltpu
from jax.sharding import PartitionSpec as P

MOST = 4096
FILL = -4.0
MESH = pl.DeviceIdType.MESH
F32 = jnp.float32
BF16 = jnp.bfloat16
I32 = jnp.int32


def nt(a, b):
    return lax.dot_general(a, b, (((1,), (1,)), ((), ())), preferred_element_type=F32)


def place(nq, at, s):
    if at > nq - 1 - at:
        at, s = nq - 1 - at, nq - 1 - s
    d = abs(s - at)
    if d > at:
        return at + d
    return 2 * d - 1 if s < at else 2 * d


def send_order(nq, q):
    up = list(range(2 * nq - 1, 2 * q + 1, -1))
    down = list(range(0, 2 * q))
    if len(up) > 4:
        up = up[:-3] + [2 * q + 3, 2 * q + 2, 2 * q + 4]
    if len(down) > 4:
        down = down[:-3] + [2 * q - 2, 2 * q - 1, 2 * q - 3]
    return up, down


def windows(nq, q):
    return list(range(nq)) if q >= nq // 2 else list(range(nq - 1, -1, -1))


def sends_after(nq, q, step):
    def ready(step):
        packed = windows(nq, q)[: step + 1]
        out = []
        for way in send_order(nq, q):
            for h in way:
                if h // 2 not in packed:
                    break
                out.append(h)
        return out

    before = ready(step - 1) if step else []
    return [h for h in ready(step) if h not in before]


def kernel(
    n, emb_in, cl_in, tp_in, out_ref,
    emb, cl, tp, packed, Q, E, idm, IDS, MSG, MSGR, top, racc, cacc, rid, qid,
    fetch_s, src_s, fx1_s, fx2_s, mr, er, y_s, y_r, c_s, c_r, d_s, d_r, ids_s, ids_r, msg_s, msg_r,
):
    nq = n // 4
    rows, width = emb.shape
    piece = rows // n
    cr = 2 * piece
    halves = 2 * nq
    wide = 4 * cr
    blk, split = lax.axis_index("blk"), lax.axis_index("split")
    me = blk * 2 + split
    q = blk // 2
    r = lax.rem(blk, 2) * 2 + split

    def dev(index):
        return {"blk": index // 2, "split": lax.rem(index, 2)}

    rc = lax.rem(blk, 2) * 2 + (1 - split)
    ry = lax.rem(r + 2, 4)
    rd = lax.rem(rc + 2, 4)
    core, across = 4 * q + rc, 4 * q + ry

    fetch = [
        pltpu.make_async_copy(src, dst, fetch_s.at[i])
        for i, (src, dst) in enumerate(((tp_in, tp), (cl_in, cl), (emb_in, emb)))
    ]
    for copy in fetch:
        copy.start()

    barrier = pltpu.get_barrier_semaphore()

    @pl.loop(1, n)
    def _(o):
        pl.semaphore_signal(
            barrier, inc=1, device_id=dev(lax.rem(me + o, n)), device_id_type=MESH
        )

    shift = rows.bit_length() - 1
    fetch[0].wait()
    dest = lax.shift_right_logical(tp[...], shift)
    hit = lax.broadcasted_iota(I32, (n, rows), 0) == dest
    hot = jnp.where(hit, 1.0, 0.0)
    lanes = 128
    before = jnp.where(
        lax.broadcasted_iota(I32, (lanes, lanes), 0) < lax.broadcasted_iota(I32, (lanes, lanes), 1), 1.0, 0.0
    ).astype(BF16)
    carry = jnp.zeros((n, 1), F32)
    ranks = []
    for b in range(rows // lanes):
        some = hot[:, b * lanes : (b + 1) * lanes]
        count = jnp.dot(some.astype(BF16), before, preferred_element_type=F32) + carry
        ranks.append(jnp.sum(some * count, axis=0, keepdims=True))
        carry = carry + jnp.sum(some, axis=1, keepdims=True)
    rank = jnp.concatenate(ranks, axis=1).astype(I32)
    key = dest * piece + rank
    i0 = lax.broadcasted_iota(I32, (2 * cr, rows), 0)

    def permutation(w):
        return jnp.where(i0 == key - 2 * cr * w, 1.0, 0.0).astype(BF16)

    def pack(step):
        w = jnp.where(q >= nq // 2, step, nq - 1 - step)
        x = jnp.dot(permutation(w), emb[...], preferred_element_type=F32)
        x = x * lax.rsqrt(jnp.sum(x * x, axis=1, keepdims=True) + 1e-06)
        packed[pl.ds(2 * w, 2)] = x.astype(BF16).reshape(2, cr, width)

    fetch[1].wait()
    fetch[2].wait()
    pack(0)
    labels = jnp.broadcast_to(cl[...].astype(F32), (8, rows)).astype(BF16)
    none = jnp.full((1, cr), -1, I32)
    padded = jnp.concatenate(
        [none] + [nt(labels, permutation(w)).astype(I32)[0:1] for w in range(nq)] + [none], axis=1
    )
    for w in range(nq):
        idm[w] = padded[:, 2 * cr * w : 2 * cr * w + wide]
    pl.semaphore_wait(barrier, n - 1)

    def remote(src, dst, s_sem, r_sem, index):
        return pltpu.make_async_remote_copy(
            src_ref=src, dst_ref=dst, send_sem=s_sem, recv_sem=r_sem,
            device_id=dev(index), device_id_type=MESH,
        )

    def ids_copy(o):
        to = lax.rem(me + o, n)
        return remote(idm.at[to // 4], IDS.at[me], ids_s.at[o], ids_r.at[me], to)

    def ids_in(o):
        frm = lax.rem(me + o, n)
        return remote(idm.at[0], IDS.at[frm], ids_s.at[o], ids_r.at[frm], frm)

    for o in range(1, n):
        ids_copy(o).start()

    flip = q > nq - 1 - q

    def source(j):
        m = jnp.minimum(q, nq - 1 - q)
        d = (j + 1) // 2
        near = jnp.where(lax.rem(j, 2) == 1, m - d, m + d)
        s = jnp.where(j <= 2 * m, near, j)
        return jnp.where(flip, nq - 1 - s, s)

    def early_slot(j):
        return 2 + (nq - 1 - j)

    def late_slot(at, s):
        turn = at > nq - 1 - at
        m = jnp.minimum(at, nq - 1 - at)
        sm = jnp.where(turn, nq - 1 - s, s)
        d = jnp.abs(sm - m)
        return nq + jnp.where(d <= m, jnp.where(sm < m, 2 * d - 1, 2 * d), m + d)

    def own_send(h, at):
        t, k = h // 2, h % 2
        e = t - 1 + 2 * k
        near = e if (at < t) == (e < t) else t
        if not 0 <= e < nq:
            near = t
        if at == t:
            near = e
        elif at == e:
            near = t
        if near == at or not 0 <= near < nq:
            return None
        if near == t:
            return remote(packed.at[h], Q.at[at, k, r], src_s.at[h], mr.at[k, at], 4 * t + r)
        j = place(nq, near, at)
        to = nq + j if at == t else early_slot(j)
        return remote(packed.at[h], E.at[to], src_s.at[h], er.at[to], 4 * near + r)

    def y_copy(k, s):
        return remote(Q.at[s, k, r], Q.at[s, k, r], y_s.at[k, s], y_r.at[k, s], across)

    def c_copy(k, s):
        return remote(Q.at[s, k, r], Q.at[s, k, r], c_s.at[k, s], c_r.at[k, s], core)

    def diag(k, s):
        there = Q.at[s, k, ry]
        return remote(there, there, d_s.at[k, s], d_r.at[k, s], core)

    def y_in(k, s):
        there = Q.at[s, k, ry]
        return remote(there, there, y_s.at[k, s], y_r.at[k, s], across)

    def c_in(k, s):
        there = Q.at[s, k, rc]
        return remote(there, there, c_s.at[k, s], c_r.at[k, s], core)

    def d_in(k, s):
        there = Q.at[s, k, rd]
        return remote(there, there, d_s.at[k, s], d_r.at[k, s], core)

    def mine_in(k, s):
        there = Q.at[s, k, r]
        return remote(there, there, y_s.at[k, s], mr.at[k, s], across)

    def ext_in(at):
        there = E.at[at]
        return remote(there, there, src_s.at[0], er.at[at], across)

    def below(s):
        return jnp.where(s < q, 1, 0)

    def inner(e):
        return jnp.where(e == 1, q < nq - 1, q > 0)

    def pass_mine(j):
        s = source(j)
        e = below(s)
        return remote(
            E.at[early_slot(j)], Q.at[s, 1 - e, r], fx1_s.at[s], mr.at[1 - e, s], me + 8 * e - 4
        )

    def pass_ext(j):
        s = source(j)
        e = below(s)
        to = late_slot(q + 2 * e - 1, s)
        return remote(Q.at[s, e, r], E.at[to], fx2_s.at[s], er.at[to], me + 8 * e - 4)

    def item(t):
        v = t - 3
        last = jnp.logical_or(t == 2, t == halves - 1)
        j = jnp.where(t < 2, 0, jnp.where(last, nq - 1, 1 + v // 2))
        second = jnp.where(t < 2, t, jnp.where(last, t != 2, lax.rem(v, 2)))
        s = source(j)
        e = below(s)
        return s, jnp.where(t < 2, t, jnp.where(second == 1, 1 - e, e))

    def place_of(t):
        return 0 if t < 2 else nq - 1 if t in (2, halves - 1) else 1 + (t - 3) // 2

    def start_all(at, halves_out):
        for h in halves_out:
            copy = own_send(h, at)
            if copy is not None:
                copy.start()

    for step in range(nq):
        if step:
            pack(step)
        for at in range(nq):

            @pl.when(q == at)
            def _():
                start_all(at, sends_after(nq, at, step))
                if windows(nq, at)[step] == at:
                    for k in (0, 1):
                        Q[at, k, r] = packed[2 * at + k]
                        y_copy(k, at).start()
                        c_copy(k, at).start()

    E[0] = packed[jnp.maximum(2 * q - 1, 0)]
    E[1] = packed[jnp.minimum(2 * q + 2, halves - 1)]

    @pl.when(jnp.logical_or(q == 0, q == nq - 1))
    def _():
        for at in range(2, nq + 1):
            E[at] = jnp.zeros((cr, width), BF16)

    @pl.loop(1, n)
    def _(o):
        ids_in(o).wait_recv()

    IDS[me] = idm[q]

    for p in range(4):
        for s in range(nq):
            for k in (0, 1):
                qid[2 * s + k, 0:1, cr * p : cr * (p + 1)] = IDS[4 * s + p, :, cr * (k + 1) : cr * (k + 2)]

    def spread(row):
        return jnp.broadcast_to(row, (128, row.shape[1])).T

    for j in range(nq):
        rid[j] = spread(IDS[4 * source(j) + r, :, cr : 3 * cr])

    def ext_ids(s, upper):
        low, high = IDS[4 * s + r, :, 0:cr], IDS[4 * s + r, :, 3 * cr : 4 * cr]
        return jnp.where(upper == 1, high, low)

    ext_rows = [ext_ids(q, 0), ext_ids(q, 1)]
    for j in range(nq - 1, 0, -1):
        s = source(j)
        ext_rows.append(ext_ids(s, below(s)))
    for j in range(1, nq):
        s = source(j)
        ext_rows.append(ext_ids(s, 1 - below(s)))
    for g in range(nq):
        rid[nq + g] = spread(jnp.concatenate(ext_rows[2 * g : 2 * g + 2], axis=1))
    racc[...] = jnp.full(racc.shape, FILL, F32)
    cacc[...] = jnp.full(cacc.shape, FILL, F32)

    lane = lax.broadcasted_iota(I32, (2 * cr, 128), 1)
    sub = lax.broadcasted_iota(I32, (2 * cr, 128), 0)

    def pair(t):
        return t if isinstance(t, tuple) else item(t)

    def scores_of(at, t, side):
        if at < nq:
            left = Q[source(at), :, r].reshape(2 * cr, width)
        elif side is None:
            left = E[2 * (at - nq) : 2 * (at - nq) + 2].reshape(2 * cr, width)
        else:
            left = E[2 * (at - nq) + side]
        s, k = pair(t)
        return nt(left, Q[s, k].reshape(wide, width))

    def take(at, t, scores, same, side):
        s, k = pair(t)
        at_b = 2 * s + k
        if same:
            own = jnp.logical_and(sub >= k * cr, sub < (k + 1) * cr)
            twin = jnp.where(own, sub + (r - k) * cr, -1) - lane
        ats = [slice(128 * w, 128 * (w + 1)) for w in range(wide // 128)]
        high = [cacc[at_b, :, at_w] for at_w in ats]
        step = min(64, cr)
        for x in range(0, scores.shape[0], step):
            base = x if side is None else side * cr + x
            part, there = slice(base, base + step), slice(x, x + step)
            col = rid[at, part]
            acc = racc[at, part]
            for w, at_w in enumerate(ats):
                keep = col == qid[at_b, 0:1, at_w]
                if same:
                    keep = jnp.logical_and(keep, twin[part] != 128 * w)
                block = jnp.where(keep, scores[there, at_w], FILL)
                acc = jnp.maximum(acc, block)
                high[w] = jnp.maximum(high[w], jnp.max(block.reshape(step // 8, 8, 128), axis=0))
            racc[at, part] = acc
        for w, at_w in enumerate(ats):
            cacc[at_b, :, at_w] = high[w]

    def tiles(work, side=None):
        work = [(at, t) for at, ts in work for t in ts]
        for x in range(0, len(work), 8):
            part = work[x : x + 8]
            scores = [scores_of(at, t, side) for at, t in part]
            for (at, t), one in zip(part, scores):
                take(at, t, one, at < nq and place_of(t) == at, side)

    def widen_next(copy, j):
        @pl.when(inner(below(source(j))))
        def _():
            if copy is pass_mine:
                ext_in(early_slot(j)).wait_recv()
            copy(j).start()

    half = nq // 2
    for i in range(halves + 2):
        if 2 <= i < halves:
            s, k = item(i)
            mine_in(k, s).wait_recv()
            y_copy(k, s).start()
            c_copy(k, s).start()
        if i == halves:
            tiles([(nq - 1, range(halves - 2))])
        if 1 <= i <= halves:
            s, k = item(i - 1)
            y_in(k, s).wait_recv()
            diag(k, s).start()
        if i == 2:
            widen_next(pass_mine, nq - 1)
        if i == 4:
            for j in range(nq - 2, 0, -1):
                widen_next(pass_mine, j)
            for at in range(nq):

                @pl.when(q == at)
                def _():
                    start_all(at, (2 * at + 1, 2 * at))

            widen_next(pass_ext, nq - 1)
            widen_next(pass_ext, 1)
        if 5 <= i < halves - 1 and i % 2 == 1:
            widen_next(pass_ext, i // 2)
        if i >= 2:
            t = i - 2
            s, k = item(t)
            c_in(k, s).wait_recv()
            d_in(k, s).wait_recv()
            work = []
            if i == 3:
                work.append((0, (0, 1)))
            if i % 2 == 1:
                if 5 <= i < halves:
                    work.append(((i - 3) // 2, [u for u in range(t + 1) if u != 2]))
                work.append((nq, (t - 1, t)))
            elif 6 <= i:
                work.append(((i - 4) // 2, (t,)))
            if i >= halves - 2:
                first = i == halves - 2
                work += [(nq + g, range(t + 1) if first else (t,)) for g in range(1, half)]
            if i >= halves:
                work.append((nq - 1, (t,)))
            if i > halves - 2:
                work.append((nq + half, (t,)))
            tiles(work)
            if i == halves - 2:
                ext_in(nq + 1).wait_recv()
                tiles([(nq + half, range(t + 1))])
    def settle(first, last):
        best = jnp.max(racc[first:last].reshape(2 * (last - first) * cr, 128).T, axis=0, keepdims=True)
        for at in range(2 * (last - first)):
            top[2 * first + at] = best[:, at * cr : (at + 1) * cr]

    settle(0, nq + half + 1)

    last_items = range(halves)
    if nq - half == 2:
        e = below(source(nq - 1))
        last_items = [(s, e) for s in range(nq)]
        last_items += [(jnp.where(e == 1, s, jnp.minimum(s, q)), 1) for s in range(half)]
    for g in range(half + 1, nq):
        for side in (0, 1):
            ext_in(2 * g + side).wait_recv()
        tiles([(nq + g, last_items)])

    settle(nq + half + 1, 2 * nq)
    fill = jnp.full((1, cr), FILL, F32)
    for s in range(nq):
        e = below(s)
        own = q == s
        late = late_slot(q, s)
        early = early_slot(late - nq)
        low = top[halves + jnp.where(own, 0, jnp.where(e == 1, late, early))]
        high = top[halves + jnp.where(own, 1, jnp.where(e == 1, early, late))]
        for p in range(4):
            same = p == r
            found = [jnp.where(same, low, fill)]
            for k in (0, 1):
                column = jnp.max(cacc[2 * s + k, :, cr * p : cr * (p + 1)], axis=0, keepdims=True)
                mine = top[2 * jnp.where(own, 0, late - nq) + k]
                found.append(jnp.maximum(column, jnp.where(same, mine, fill)))
            found.append(jnp.where(same, high, fill))
            MSG[4 * s + p] = jnp.concatenate(found, axis=1)

    def msg_copy(o):
        to = lax.rem(me + o, n)
        return remote(MSG.at[to], MSGR.at[me], msg_s.at[o], msg_r.at[me], to)

    @pl.loop(1, n)
    def _(o):
        msg_copy(o).start()

    MSGR[me] = MSG[me]

    for at in range(nq):

        @pl.when(q == at)
        def _():
            for h in range(halves):
                copy = own_send(h, at)
                if copy is not None:
                    copy.wait_send()

    @pl.loop(1, n)
    def _(o):
        ids_copy(o).wait_send()

    @pl.loop(0, halves)
    def _(t):
        s, k = item(t)
        y_copy(k, s).wait_send()
        c_copy(k, s).wait_send()
        diag(k, s).wait_send()

    @pl.loop(1, nq)
    def _(j):
        @pl.when(inner(below(source(j))))
        def _():
            pass_mine(j).wait_send()
            pass_ext(j).wait_send()

    bits = cr.bit_length() - 1
    hot_l = jnp.where(
        lax.broadcasted_iota(I32, (cr, rows), 0) == (key & (cr - 1)), 1.0, 0.0
    ).astype(BF16)
    at_h = lax.broadcasted_iota(I32, (halves, rows), 0) == lax.shift_right_logical(key, bits)

    @pl.loop(1, n)
    def _(o):
        frm = lax.rem(me + o, n)
        remote(MSG.at[0], MSGR.at[frm], msg_s.at[o], msg_r.at[frm], frm).wait_recv()

    table = []
    for h in range(halves):
        t, k = h // 2, h % 2
        e = t - 1 + 2 * k
        found = MSGR[4 * t, :, (k + 1) * cr : (k + 2) * cr]
        for p in range(1, 4):
            found = jnp.maximum(found, MSGR[4 * t + p, :, (k + 1) * cr : (k + 2) * cr])
        if 0 <= e < nq:
            off = 3 * cr * (1 - k)
            found = jnp.maximum(found, MSGR[4 * e + r, :, off : off + cr])
        table.append(found)
    table = jnp.concatenate(table, axis=0)
    hi = table.astype(BF16)
    rest = table - hi.astype(F32)
    mid = rest.astype(BF16)
    low = (rest - mid.astype(F32)).astype(BF16)
    got = jnp.dot(hi, hot_l, preferred_element_type=F32)
    got += jnp.dot(mid, hot_l, preferred_element_type=F32)
    got += jnp.dot(low, hot_l, preferred_element_type=F32)
    out_ref[...] = jnp.max(jnp.where(at_h, got, FILL), axis=0, keepdims=True)

    @pl.loop(1, n)
    def _(o):
        msg_copy(o).wait_send()


def body(n, embeddings, cluster_of, target_pos):
    rows, width = embeddings.shape
    nq, cr = n // 4, 2 * rows // n
    assert MOST <= 4 * rows and n % 8 == 0
    dma = pltpu.SemaphoreType.DMA
    out = pl.pallas_call(
        functools.partial(kernel, n),
        out_shape=jax.ShapeDtypeStruct((1, rows), F32),
        in_specs=[pl.BlockSpec(memory_space=pl.ANY)] * 3,
        out_specs=pl.BlockSpec(memory_space=pltpu.VMEM),
        scratch_shapes=[
            pltpu.VMEM((rows, width), BF16),
            pltpu.VMEM((1, rows), I32),
            pltpu.VMEM((1, rows), I32),
            pltpu.VMEM((2 * nq, cr, width), BF16),
            pltpu.VMEM((nq, 2, 4, cr, width), BF16),
            pltpu.VMEM((2 * nq, cr, width), BF16),
            pltpu.VMEM((nq, 1, 4 * cr), I32),
            pltpu.VMEM((n, 1, 4 * cr), I32),
            pltpu.VMEM((n, 1, 4 * cr), F32),
            pltpu.VMEM((n, 1, 4 * cr), F32),
            pltpu.VMEM((4 * nq, 1, cr), F32),
            pltpu.VMEM((2 * nq, 2 * cr, 128), F32),
            pltpu.VMEM((2 * nq, 8, 4 * cr), F32),
            pltpu.VMEM((2 * nq, 2 * cr, 128), I32),
            pltpu.VMEM((2 * nq, 8, 4 * cr), I32),
            dma((3,)), dma((2 * nq,)), dma((nq,)), dma((nq,)), dma((2, nq)), dma((2 * nq,)),
            dma((2, nq)), dma((2, nq)), dma((2, nq)), dma((2, nq)), dma((2, nq)), dma((2, nq)),
            dma((n,)), dma((n,)), dma((n,)), dma((n,)),
        ],
        compiler_params=pltpu.CompilerParams(
            collective_id=0, has_side_effects=True, vmem_limit_bytes=60 * 2**20
        ),
    )(embeddings, cluster_of.reshape(1, rows), target_pos.reshape(1, rows))
    return out.reshape(rows)


def solution(mesh):
    n = mesh.shape["blk"] * mesh.shape["split"]
    spec = P(("groups", "blk", "split"))
    return jax.shard_map(
        functools.partial(body, n),
        mesh=mesh,
        in_specs=(P(("groups", "blk", "split"), None), spec, spec),
        out_specs=spec,
        check_vma=False,
    )
```

```python
import functools

import jax
import jax.numpy as jnp
from jax import lax
from jax.experimental import pallas as pl
from jax.experimental.pallas import tpu as pltpu
from jax.sharding import PartitionSpec as P

MOST = 4096
FILL = -4.0
MESH = pl.DeviceIdType.MESH
F32 = jnp.float32
BF16 = jnp.bfloat16
I32 = jnp.int32


def nt(a, b):
    return lax.dot_general(a, b, (((1,), (1,)), ((), ())), preferred_element_type=F32)


def place(nq, at, s):
    if at > nq - 1 - at:
        at, s = nq - 1 - at, nq - 1 - s
    d = abs(s - at)
    if d > at:
        return at + d
    return 2 * d - 1 if s < at else 2 * d


def send_order(nq, q):
    up = list(range(2 * nq - 1, 2 * q + 1, -1))
    down = list(range(0, 2 * q))
    if len(up) > 4:
        up = up[:-3] + [2 * q + 3, 2 * q + 2, 2 * q + 4]
    if len(down) > 4:
        down = down[:-3] + [2 * q - 2, 2 * q - 1, 2 * q - 3]
    return up, down


def windows(nq, q):
    return list(range(nq)) if q >= nq // 2 else list(range(nq - 1, -1, -1))


def sends_after(nq, q, step):
    def ready(step):
        packed = windows(nq, q)[: step + 1]
        out = []
        for way in send_order(nq, q):
            for h in way:
                if h // 2 not in packed:
                    break
                out.append(h)
        return out

    before = ready(step - 1) if step else []
    return [h for h in ready(step) if h not in before]


def kernel(
    n, emb_in, cl_in, tp_in, out_ref,
    emb, cl, tp, packed, Q, E, idm, IDS, MSG, MSGR, top, racc, cacc, rid, qid,
    fetch_s, src_s, fx1_s, fx2_s, mr, er, y_s, y_r, c_s, c_r, d_s, d_r, ids_s, ids_r, msg_s, msg_r,
):
    nq = n // 4
    rows, width = emb.shape
    piece = rows // n
    cr = 2 * piece
    halves = 2 * nq
    wide = 4 * cr
    blk, split = lax.axis_index("blk"), lax.axis_index("split")
    me = blk * 2 + split
    q = blk // 2
    r = lax.rem(blk, 2) * 2 + split

    def dev(index):
        return {"blk": index // 2, "split": lax.rem(index, 2)}

    rc = lax.rem(blk, 2) * 2 + (1 - split)
    ry = lax.rem(r + 2, 4)
    rd = lax.rem(rc + 2, 4)
    core, across = 4 * q + rc, 4 * q + ry

    fetch = [
        pltpu.make_async_copy(src, dst, fetch_s.at[i])
        for i, (src, dst) in enumerate(((tp_in, tp), (cl_in, cl), (emb_in, emb)))
    ]
    for copy in fetch:
        copy.start()

    barrier = pltpu.get_barrier_semaphore()

    @pl.loop(1, n)
    def _(o):
        pl.semaphore_signal(
            barrier, inc=1, device_id=dev(lax.rem(me + o, n)), device_id_type=MESH
        )

    shift = rows.bit_length() - 1
    fetch[0].wait()
    dest = lax.shift_right_logical(tp[...], shift)
    hit = lax.broadcasted_iota(I32, (n, rows), 0) == dest
    hot = jnp.where(hit, 1.0, 0.0)
    lanes = 128
    before = jnp.where(
        lax.broadcasted_iota(I32, (lanes, lanes), 0) < lax.broadcasted_iota(I32, (lanes, lanes), 1), 1.0, 0.0
    ).astype(BF16)
    carry = jnp.zeros((n, 1), F32)
    ranks = []
    for b in range(rows // lanes):
        some = hot[:, b * lanes : (b + 1) * lanes]
        count = jnp.dot(some.astype(BF16), before, preferred_element_type=F32) + carry
        ranks.append(jnp.sum(some * count, axis=0, keepdims=True))
        carry = carry + jnp.sum(some, axis=1, keepdims=True)
    rank = jnp.concatenate(ranks, axis=1).astype(I32)
    key = dest * piece + rank
    i0 = lax.broadcasted_iota(I32, (2 * cr, rows), 0)

    def permutation(w):
        return jnp.where(i0 == key - 2 * cr * w, 1.0, 0.0).astype(BF16)

    def pack(step):
        w = jnp.where(q >= nq // 2, step, nq - 1 - step)
        x = jnp.dot(permutation(w), emb[...], preferred_element_type=F32)
        x = x * lax.rsqrt(jnp.sum(x * x, axis=1, keepdims=True) + 1e-06)
        packed[pl.ds(2 * w, 2)] = x.astype(BF16).reshape(2, cr, width)

    fetch[1].wait()
    fetch[2].wait()
    pack(0)
    labels = jnp.broadcast_to(cl[...].astype(F32), (8, rows)).astype(BF16)
    none = jnp.full((1, cr), -1, I32)
    padded = jnp.concatenate(
        [none] + [nt(labels, permutation(w)).astype(I32)[0:1] for w in range(nq)] + [none], axis=1
    )
    for w in range(nq):
        idm[w] = padded[:, 2 * cr * w : 2 * cr * w + wide]
    pl.semaphore_wait(barrier, n - 1)

    def remote(src, dst, s_sem, r_sem, index):
        return pltpu.make_async_remote_copy(
            src_ref=src, dst_ref=dst, send_sem=s_sem, recv_sem=r_sem,
            device_id=dev(index), device_id_type=MESH,
        )

    def ids_copy(o):
        to = lax.rem(me + o, n)
        return remote(idm.at[to // 4], IDS.at[me], ids_s.at[o], ids_r.at[me], to)

    def ids_in(o):
        frm = lax.rem(me + o, n)
        return remote(idm.at[0], IDS.at[frm], ids_s.at[o], ids_r.at[frm], frm)

    for o in range(1, n):
        ids_copy(o).start()

    flip = q > nq - 1 - q

    def source(j):
        m = jnp.minimum(q, nq - 1 - q)
        d = (j + 1) // 2
        near = jnp.where(lax.rem(j, 2) == 1, m - d, m + d)
        s = jnp.where(j <= 2 * m, near, j)
        return jnp.where(flip, nq - 1 - s, s)

    def early_slot(j):
        return 2 + (nq - 1 - j)

    def late_slot(at, s):
        turn = at > nq - 1 - at
        m = jnp.minimum(at, nq - 1 - at)
        sm = jnp.where(turn, nq - 1 - s, s)
        d = jnp.abs(sm - m)
        return nq + jnp.where(d <= m, jnp.where(sm < m, 2 * d - 1, 2 * d), m + d)

    def own_send(h, at):
        t, k = h // 2, h % 2
        e = t - 1 + 2 * k
        near = e if (at < t) == (e < t) else t
        if not 0 <= e < nq:
            near = t
        if at == t:
            near = e
        elif at == e:
            near = t
        if near == at or not 0 <= near < nq:
            return None
        if near == t:
            return remote(packed.at[h], Q.at[at, k, r], src_s.at[h], mr.at[k, at], 4 * t + r)
        j = place(nq, near, at)
        to = nq + j if at == t else early_slot(j)
        return remote(packed.at[h], E.at[to], src_s.at[h], er.at[to], 4 * near + r)

    def y_copy(k, s):
        return remote(Q.at[s, k, r], Q.at[s, k, r], y_s.at[k, s], y_r.at[k, s], across)

    def c_copy(k, s):
        return remote(Q.at[s, k, r], Q.at[s, k, r], c_s.at[k, s], c_r.at[k, s], core)

    def diag(k, s):
        there = Q.at[s, k, ry]
        return remote(there, there, d_s.at[k, s], d_r.at[k, s], core)

    def y_in(k, s):
        there = Q.at[s, k, ry]
        return remote(there, there, y_s.at[k, s], y_r.at[k, s], across)

    def c_in(k, s):
        there = Q.at[s, k, rc]
        return remote(there, there, c_s.at[k, s], c_r.at[k, s], core)

    def d_in(k, s):
        there = Q.at[s, k, rd]
        return remote(there, there, d_s.at[k, s], d_r.at[k, s], core)

    def mine_in(k, s):
        there = Q.at[s, k, r]
        return remote(there, there, y_s.at[k, s], mr.at[k, s], across)

    def ext_in(at):
        there = E.at[at]
        return remote(there, there, src_s.at[0], er.at[at], across)

    def below(s):
        return jnp.where(s < q, 1, 0)

    def inner(e):
        return jnp.where(e == 1, q < nq - 1, q > 0)

    def pass_mine(j):
        s = source(j)
        e = below(s)
        return remote(
            E.at[early_slot(j)], Q.at[s, 1 - e, r], fx1_s.at[s], mr.at[1 - e, s], me + 8 * e - 4
        )

    def pass_ext(j):
        s = source(j)
        e = below(s)
        to = late_slot(q + 2 * e - 1, s)
        return remote(Q.at[s, e, r], E.at[to], fx2_s.at[s], er.at[to], me + 8 * e - 4)

    def item(t):
        v = t - 3
        last = jnp.logical_or(t == 2, t == halves - 1)
        j = jnp.where(t < 2, 0, jnp.where(last, nq - 1, 1 + v // 2))
        second = jnp.where(t < 2, t, jnp.where(last, t != 2, lax.rem(v, 2)))
        s = source(j)
        e = below(s)
        return s, jnp.where(t < 2, t, jnp.where(second == 1, 1 - e, e))

    def place_of(t):
        return 0 if t < 2 else nq - 1 if t in (2, halves - 1) else 1 + (t - 3) // 2

    def start_all(at, halves_out):
        for h in halves_out:
            copy = own_send(h, at)
            if copy is not None:
                copy.start()

    for step in range(nq):
        if step:
            pack(step)
        for at in range(nq):

            @pl.when(q == at)
            def _():
                start_all(at, sends_after(nq, at, step))
                if windows(nq, at)[step] == at:
                    for k in (0, 1):
                        Q[at, k, r] = packed[2 * at + k]
                        y_copy(k, at).start()
                        c_copy(k, at).start()

    E[0] = packed[jnp.maximum(2 * q - 1, 0)]
    E[1] = packed[jnp.minimum(2 * q + 2, halves - 1)]

    @pl.when(jnp.logical_or(q == 0, q == nq - 1))
    def _():
        for at in range(2, nq + 1):
            E[at] = jnp.zeros((cr, width), BF16)

    @pl.loop(1, n)
    def _(o):
        ids_in(o).wait_recv()

    IDS[me] = idm[q]

    for p in range(4):
        for s in range(nq):
            for k in (0, 1):
                qid[2 * s + k, 0:1, cr * p : cr * (p + 1)] = IDS[4 * s + p, :, cr * (k + 1) : cr * (k + 2)]

    def spread(row):
        return jnp.broadcast_to(row, (128, row.shape[1])).T

    for j in range(nq):
        rid[j] = spread(IDS[4 * source(j) + r, :, cr : 3 * cr])

    def ext_ids(s, upper):
        low, high = IDS[4 * s + r, :, 0:cr], IDS[4 * s + r, :, 3 * cr : 4 * cr]
        return jnp.where(upper == 1, high, low)

    ext_rows = [ext_ids(q, 0), ext_ids(q, 1)]
    for j in range(nq - 1, 0, -1):
        s = source(j)
        ext_rows.append(ext_ids(s, below(s)))
    for j in range(1, nq):
        s = source(j)
        ext_rows.append(ext_ids(s, 1 - below(s)))
    for g in range(nq):
        rid[nq + g] = spread(jnp.concatenate(ext_rows[2 * g : 2 * g + 2], axis=1))
    racc[...] = jnp.full(racc.shape, FILL, F32)
    cacc[...] = jnp.full(cacc.shape, FILL, F32)

    lane = lax.broadcasted_iota(I32, (2 * cr, 128), 1)
    sub = lax.broadcasted_iota(I32, (2 * cr, 128), 0)

    def pair(t):
        return t if isinstance(t, tuple) else item(t)

    def scores_of(at, t, side):
        if at < nq:
            left = Q[source(at), :, r].reshape(2 * cr, width)
        elif side is None:
            left = E[2 * (at - nq) : 2 * (at - nq) + 2].reshape(2 * cr, width)
        else:
            left = E[2 * (at - nq) + side]
        s, k = pair(t)
        return nt(left, Q[s, k].reshape(wide, width))

    def take(at, t, scores, same, side):
        s, k = pair(t)
        at_b = 2 * s + k
        if same:
            own = jnp.logical_and(sub >= k * cr, sub < (k + 1) * cr)
            twin = jnp.where(own, sub + (r - k) * cr, -1) - lane
        ats = [slice(128 * w, 128 * (w + 1)) for w in range(wide // 128)]
        high = [cacc[at_b, :, at_w] for at_w in ats]
        step = min(64, cr)
        for x in range(0, scores.shape[0], step):
            base = x if side is None else side * cr + x
            part, there = slice(base, base + step), slice(x, x + step)
            col = rid[at, part]
            acc = racc[at, part]
            for w, at_w in enumerate(ats):
                keep = col == qid[at_b, 0:1, at_w]
                if same:
                    keep = jnp.logical_and(keep, twin[part] != 128 * w)
                block = jnp.where(keep, scores[there, at_w], FILL)
                acc = jnp.maximum(acc, block)
                high[w] = jnp.maximum(high[w], jnp.max(block.reshape(step // 8, 8, 128), axis=0))
            racc[at, part] = acc
        for w, at_w in enumerate(ats):
            cacc[at_b, :, at_w] = high[w]

    def tiles(work, side=None):
        work = [(at, t) for at, ts in work for t in ts]
        for x in range(0, len(work), 8):
            part = work[x : x + 8]
            scores = [scores_of(at, t, side) for at, t in part]
            for (at, t), one in zip(part, scores):
                take(at, t, one, at < nq and place_of(t) == at, side)

    def widen_next(copy, j):
        @pl.when(inner(below(source(j))))
        def _():
            if copy is pass_mine:
                ext_in(early_slot(j)).wait_recv()
            copy(j).start()

    half = nq // 2
    for i in range(halves + 2):
        if 2 <= i < halves:
            s, k = item(i)
            mine_in(k, s).wait_recv()
            y_copy(k, s).start()
            c_copy(k, s).start()
        if i == halves:
            tiles([(nq - 1, range(halves - 2))])
        if 1 <= i <= halves:
            s, k = item(i - 1)
            y_in(k, s).wait_recv()
            diag(k, s).start()
        if i == 2:
            widen_next(pass_mine, nq - 1)
        if i == 4:
            for j in range(nq - 2, 0, -1):
                widen_next(pass_mine, j)
            for at in range(nq):

                @pl.when(q == at)
                def _():
                    start_all(at, (2 * at + 1, 2 * at))

            widen_next(pass_ext, nq - 1)
            widen_next(pass_ext, 1)
        if 5 <= i < halves - 1 and i % 2 == 1:
            widen_next(pass_ext, i // 2)
        if i >= 2:
            t = i - 2
            s, k = item(t)
            c_in(k, s).wait_recv()
            d_in(k, s).wait_recv()
            work = []
            if i == 3:
                work.append((0, (0, 1)))
            if i % 2 == 1:
                if 5 <= i < halves:
                    work.append(((i - 3) // 2, (t,)))
                work.append((nq, (t,) if i > halves else (t - 1, t)))
            else:
                if 6 <= i:
                    work.append(((i - 4) // 2, (t,)))
                if 4 <= i < halves:
                    work.append(((i - 2) // 2, [u for u in range(t + 1) if u != 2]))
            if i >= 5:
                work += [(nq + g, range(t + 1) if i == 5 else (t,)) for g in range(1, half)]
            if i == halves:
                work.append((nq, (t,)))
            if i >= halves:
                work.append((nq - 1, (t,)))
            if i >= halves:
                work.append((nq + half, (t,)))
            tiles(work)
            if i == halves - 1:
                ext_in(nq + 1).wait_recv()
                tiles([(nq + half, range(t + 1))])
    def settle(first, last):
        best = jnp.max(racc[first:last].reshape(2 * (last - first) * cr, 128).T, axis=0, keepdims=True)
        for at in range(2 * (last - first)):
            top[2 * first + at] = best[:, at * cr : (at + 1) * cr]

    settle(0, nq + half + 1)

    last_items = range(halves)
    if nq - half == 2:
        e = below(source(nq - 1))
        last_items = [(s, e) for s in range(nq)]
        last_items += [(jnp.where(e == 1, s, jnp.minimum(s, q)), 1) for s in range(half)]
    for g in range(half + 1, nq):
        for side in (0, 1):
            ext_in(2 * g + side).wait_recv()
        tiles([(nq + g, last_items)])

    settle(nq + half + 1, 2 * nq)
    fill = jnp.full((1, cr), FILL, F32)
    for s in range(nq):
        e = below(s)
        own = q == s
        late = late_slot(q, s)
        early = early_slot(late - nq)
        low = top[halves + jnp.where(own, 0, jnp.where(e == 1, late, early))]
        high = top[halves + jnp.where(own, 1, jnp.where(e == 1, early, late))]
        for p in range(4):
            same = p == r
            found = [jnp.where(same, low, fill)]
            for k in (0, 1):
                column = jnp.max(cacc[2 * s + k, :, cr * p : cr * (p + 1)], axis=0, keepdims=True)
                mine = top[2 * jnp.where(own, 0, late - nq) + k]
                found.append(jnp.maximum(column, jnp.where(same, mine, fill)))
            found.append(jnp.where(same, high, fill))
            MSG[4 * s + p] = jnp.concatenate(found, axis=1)

    def msg_copy(o):
        to = lax.rem(me + o, n)
        return remote(MSG.at[to], MSGR.at[me], msg_s.at[o], msg_r.at[me], to)

    @pl.loop(1, n)
    def _(o):
        msg_copy(o).start()

    MSGR[me] = MSG[me]

    for at in range(nq):

        @pl.when(q == at)
        def _():
            for h in range(halves):
                copy = own_send(h, at)
                if copy is not None:
                    copy.wait_send()

    @pl.loop(1, n)
    def _(o):
        ids_copy(o).wait_send()

    @pl.loop(0, halves)
    def _(t):
        s, k = item(t)
        y_copy(k, s).wait_send()
        c_copy(k, s).wait_send()
        diag(k, s).wait_send()

    @pl.loop(1, nq)
    def _(j):
        @pl.when(inner(below(source(j))))
        def _():
            pass_mine(j).wait_send()
            pass_ext(j).wait_send()

    bits = cr.bit_length() - 1
    hot_l = jnp.where(
        lax.broadcasted_iota(I32, (cr, rows), 0) == (key & (cr - 1)), 1.0, 0.0
    ).astype(BF16)
    at_h = lax.broadcasted_iota(I32, (halves, rows), 0) == lax.shift_right_logical(key, bits)

    @pl.loop(1, n)
    def _(o):
        frm = lax.rem(me + o, n)
        remote(MSG.at[0], MSGR.at[frm], msg_s.at[o], msg_r.at[frm], frm).wait_recv()

    table = []
    for h in range(halves):
        t, k = h // 2, h % 2
        e = t - 1 + 2 * k
        found = MSGR[4 * t, :, (k + 1) * cr : (k + 2) * cr]
        for p in range(1, 4):
            found = jnp.maximum(found, MSGR[4 * t + p, :, (k + 1) * cr : (k + 2) * cr])
        if 0 <= e < nq:
            off = 3 * cr * (1 - k)
            found = jnp.maximum(found, MSGR[4 * e + r, :, off : off + cr])
        table.append(found)
    table = jnp.concatenate(table, axis=0)
    hi = table.astype(BF16)
    rest = table - hi.astype(F32)
    mid = rest.astype(BF16)
    low = (rest - mid.astype(F32)).astype(BF16)
    got = jnp.dot(hi, hot_l, preferred_element_type=F32)
    got += jnp.dot(mid, hot_l, preferred_element_type=F32)
    got += jnp.dot(low, hot_l, preferred_element_type=F32)
    out_ref[...] = jnp.max(jnp.where(at_h, got, FILL), axis=0, keepdims=True)

    @pl.loop(1, n)
    def _(o):
        msg_copy(o).wait_send()


def body(n, embeddings, cluster_of, target_pos):
    rows, width = embeddings.shape
    nq, cr = n // 4, 2 * rows // n
    assert MOST <= 4 * rows and n % 8 == 0
    dma = pltpu.SemaphoreType.DMA
    out = pl.pallas_call(
        functools.partial(kernel, n),
        out_shape=jax.ShapeDtypeStruct((1, rows), F32),
        in_specs=[pl.BlockSpec(memory_space=pl.ANY)] * 3,
        out_specs=pl.BlockSpec(memory_space=pltpu.VMEM),
        scratch_shapes=[
            pltpu.VMEM((rows, width), BF16),
            pltpu.VMEM((1, rows), I32),
            pltpu.VMEM((1, rows), I32),
            pltpu.VMEM((2 * nq, cr, width), BF16),
            pltpu.VMEM((nq, 2, 4, cr, width), BF16),
            pltpu.VMEM((2 * nq, cr, width), BF16),
            pltpu.VMEM((nq, 1, 4 * cr), I32),
            pltpu.VMEM((n, 1, 4 * cr), I32),
            pltpu.VMEM((n, 1, 4 * cr), F32),
            pltpu.VMEM((n, 1, 4 * cr), F32),
            pltpu.VMEM((4 * nq, 1, cr), F32),
            pltpu.VMEM((2 * nq, 2 * cr, 128), F32),
            pltpu.VMEM((2 * nq, 8, 4 * cr), F32),
            pltpu.VMEM((2 * nq, 2 * cr, 128), I32),
            pltpu.VMEM((2 * nq, 8, 4 * cr), I32),
            dma((3,)), dma((2 * nq,)), dma((nq,)), dma((nq,)), dma((2, nq)), dma((2 * nq,)),
            dma((2, nq)), dma((2, nq)), dma((2, nq)), dma((2, nq)), dma((2, nq)), dma((2, nq)),
            dma((n,)), dma((n,)), dma((n,)), dma((n,)),
        ],
        compiler_params=pltpu.CompilerParams(
            collective_id=0, has_side_effects=True, vmem_limit_bytes=60 * 2**20
        ),
    )(embeddings, cluster_of.reshape(1, rows), target_pos.reshape(1, rows))
    return out.reshape(rows)


def solution(mesh):
    n = mesh.shape["blk"] * mesh.shape["split"]
    spec = P(("groups", "blk", "split"))
    return jax.shard_map(
        functools.partial(body, n),
        mesh=mesh,
        in_specs=(P(("groups", "blk", "split"), None), spec, spec),
        out_specs=spec,
        check_vma=False,
    )
```
